32 devices in a mesh: rep: 2 (over y), seq: 4 (over z), head: 2 (over x), sub: 2 (over core).
Axes of the slice: x: 2, y: 2, z: 4, core: 2. Of those that a mesh axis runs over, the one named last changes fastest.
Arguments:
- queries: bfloat16 [4096, 2048], P(('rep', 'seq', 'sub'), 'head'), parts along dimension 0, may hold values from -1.5 to 1.5
- key_vectors: bfloat16 [4096, 2048], P(('rep', 'seq'), 'head'), parts along dimension 0, may hold values from -1.5 to 1.5
- value_vectors: bfloat16 [4096, 2048], P(('rep', 'seq'), 'head'), parts along dimension 0, may hold values from -6 to 6
- gate_bins: int32 [4096, 16], P(('rep', 'seq'), 'head'), parts along dimension 0, may hold values from 0 to 2048
- doc_lengths: int32 [6], P('rep'), parts along dimension 0, may hold values from 1 to 1536, as said below
- decay_rates: float32 [16], P('head'), may hold values from 0.15 to 86
- ridge_terms: float32 [16], P('head'), may hold values from 0.5 to 2
Outputs:
- mesa_output: bfloat16 [4096, 2048], P(('rep', 'seq', 'sub'), 'head'), parts along dimension 0
The draws below stay inside these ranges and needn't reach their ends.
There are 2 independent parts, one for each index of `rep`. The reference program is written for one: setup_inputs(seed, part) draws one part's arguments, and reference() takes and returns one part's arrays. A program takes and returns all parts, laid end to end along the dimension named above; an argument that names none is the same for every part. Nothing has to cross between parts.
Inputs may be any that keep to these rules, and one draw needn't show every extreme that they name: `doc_lengths`: the lengths sum to 2048.
All inputs are finite; a program needn't handle non-finite values.
Results may differ from the reference program's by a relative error of at most 0.001.
Values sent between devices are 32-bit elements; how exact they have to be, the bound alone decides.
No kernel may reach another device: no remote copies, remote signals or barrier semaphores. Data moves between devices by JAX's collectives and lax.ppermute only.
A program may use at most 64 MiB of HBM per device.

```python
import math
import jax
import jax.numpy as jnp
from jax import lax

H = 16
DK = 128
DV = 128
S_DEV = 512
ITERS = 4
INPUT_LENGTH = 2048


def document_layout(key):
    slot_key, split_key, run_key = jax.random.split(jax.random.fold_in(key, 51), 3)
    largest = INPUT_LENGTH * 3 // 4
    remainder = INPUT_LENGTH - largest
    largest_slot = jax.random.randint(slot_key, (), 0, 3, jnp.int32)
    first_other = jax.random.randint(split_key, (), 1, remainder, jnp.int32)
    second_other = (remainder - first_other).astype(jnp.int32)
    largest_len = jnp.full((), largest, jnp.int32)
    option_zero = jnp.stack([largest_len, first_other, second_other])
    option_one = jnp.stack([first_other, largest_len, second_other])
    option_two = jnp.stack([first_other, second_other, largest_len])
    doc_sizes = jnp.where(largest_slot == 0, option_zero, jnp.where(largest_slot == 1, option_one, option_two))
    largest_start = jnp.where(largest_slot == 0, 0, jnp.where(largest_slot == 1, first_other, first_other + second_other))
    run_offset = jax.random.randint(run_key, (), 1, INPUT_LENGTH // 2 + 1, jnp.int32)
    run_start = (largest_start + run_offset).astype(jnp.int32)
    return (doc_sizes.astype(jnp.int32), run_start)


def draw_doc_lengths(key, part):
    layout = document_layout(key)
    return layout[0]


def draw_key_vectors(key, part):
    leading_probe_vector, trailing_probe_vector = jax.random.split(jax.random.fold_in(key, 11))
    column_scales = jnp.exp(jax.random.uniform(leading_probe_vector, (H * DK,), jnp.float32, jnp.log(0.01), jnp.log(0.3)))
    lookup_cells = jnp.clip(jax.random.normal(trailing_probe_vector, (INPUT_LENGTH, H * DK), jnp.float32), -5.0, 5.0)
    return (lookup_cells * column_scales[None, :]).astype(jnp.bfloat16)


def draw_decay_rates(key, part):
    leading_probe_vector, trailing_probe_vector, third_key = jax.random.split(jax.random.fold_in(key, 23), 3)
    slow_rates = jnp.exp(jax.random.uniform(leading_probe_vector, (H,), jnp.float32, jnp.log(0.15), jnp.log(0.7)))
    fast_rates = jnp.exp(jax.random.uniform(trailing_probe_vector, (H,), jnp.float32, jnp.log(INPUT_LENGTH / 64.0), jnp.log(INPUT_LENGTH / 24.0)))
    slow_share = 0.5
    chosen = jax.random.uniform(third_key, (H,), jnp.float32) < slow_share
    return jnp.where(chosen, slow_rates, fast_rates).astype(jnp.float32)


def draw_gate_bins(key, part):
    layout = document_layout(key)
    run_start = layout[1]
    run_length = INPUT_LENGTH // 8
    bin_key, spike_key = jax.random.split(jax.random.fold_in(key, 37))
    lookup_cells = jax.random.randint(bin_key, (INPUT_LENGTH, H), 0, 3, jnp.int32)
    spike_draws = jax.random.randint(spike_key, (2,), 0, INPUT_LENGTH - 2 * run_length, jnp.int32)
    spike_indices = spike_draws + jnp.where(spike_draws >= run_start, 2 * run_length, 0).astype(jnp.int32)
    element_offsets = jnp.arange(INPUT_LENGTH, dtype=jnp.int32)
    spike_instances = jnp.any(element_offsets[:, None] == spike_indices[None, :], axis=1)
    in_run = (element_offsets >= run_start) & (element_offsets < run_start + run_length)
    binned = jnp.where(spike_instances[:, None], INPUT_LENGTH, lookup_cells)
    binned = jnp.where(in_run[:, None], 0, binned)
    return binned.astype(jnp.int32)


def block_scale(own_key, extent, cuts, low, top_value):
    factor_of, own = 1.0, jax.random.fold_in(own_key, 6)
    for axis_at, blocks in cuts:
        draws = jnp.exp(jax.random.uniform(jax.random.fold_in(own, axis_at), (blocks,), jnp.float32, low / len(cuts), top_value / len(cuts)))
        factor_of = factor_of * jnp.repeat(draws, extent[axis_at] // blocks).reshape([-1 if axis == axis_at else 1 for axis in range(len(extent))])
    return factor_of


def noise(rng, shape, scale, most, shards=(), kind=jnp.bfloat16):
    drawn = jax.random.normal(rng, shape, jnp.float32) * scale
    if len(shards) > 0:
        drawn = block_scale(rng, shape, shards, -0.22, 0.18) * drawn
    return jnp.clip(drawn, min=-most, max=most).astype(kind)


def setup_inputs(seed: int = 0, part: int = 0) -> dict:
    streams_of = jax.random.split(jax.random.key(seed), 8)
    part_splits = jax.random.split(jax.random.fold_in(streams_of[7], part), 8)
    return {
        "queries": noise(part_splits[0], (INPUT_LENGTH, H * DK), 0.25, 1.5, ((0, 8), (1, 2))),
        "key_vectors": draw_key_vectors(jax.random.fold_in(jax.random.fold_in(streams_of[7], part), 71), part),
        "value_vectors": noise(part_splits[2], (INPUT_LENGTH, H * DV), 1.0, 6.0, ((0, 4), (1, 2))),
        "gate_bins": draw_gate_bins(jax.random.fold_in(jax.random.fold_in(streams_of[7], part), 71), part),
        "doc_lengths": draw_doc_lengths(jax.random.fold_in(jax.random.fold_in(streams_of[7], part), 71), part),
        "decay_rates": draw_decay_rates(jax.random.fold_in(streams_of[7], 71), part),
        "ridge_terms": jnp.clip(jnp.exp(math.log(2.0) - 1.3862944 * jax.random.uniform(streams_of[6], (H,), jnp.float32) ** block_scale(streams_of[6], (H,), ((0, 2),), -0.2, 0.2)), 0.5, 2.0),
    }


highest = lax.Precision.HIGHEST
guard = 1e-6


def gate_weights(cumulative, doc_ids, query_cum, query_doc, query_pos, prior_doc):
    key_position = jnp.arange(cumulative.shape[0], dtype=jnp.int32)
    allowed = (key_position[None, :] <= query_pos[:, None]) & (doc_ids[None, :] == query_doc[:, None])
    spread_log = query_cum.T[:, :, None] - cumulative.T[:, None, :]
    weights = jnp.where(allowed[None], jnp.exp(jnp.minimum(spread_log, 0.0)), 0.0)
    carried = jnp.where((query_doc == prior_doc)[None, :], jnp.exp(query_cum.T), 0.0)
    return weights, carried


def solve_and_read(query_all, key_all, value_all, weights, carried, gram_state, memory, ridge_terms):
    def apply_system(direction):
        correlation = jnp.einsum('hrd,hsd->hrs', direction, key_all, precision=highest) * weights
        within = jnp.einsum('hrs,hsd->hrd', correlation, key_all, precision=highest)
        earlier = jnp.einsum('hrd,hed->hre', direction, gram_state, precision=highest)
        return carried[..., None] * earlier + within + ridge_terms[:, None, None] * direction

    solution = jnp.zeros_like(query_all)
    residual = query_all
    direction = query_all
    energy = jnp.sum(residual * residual, axis=-1)
    for iteration in range(ITERS):
        product = apply_system(direction)
        stepsize = energy / (jnp.sum(direction * product, axis=-1) + guard)
        solution = solution + stepsize[..., None] * direction
        residual = residual - stepsize[..., None] * product
        energy_next = jnp.sum(residual * residual, axis=-1)
        direction = residual + (energy_next / (energy + guard))[..., None] * direction
        energy = energy_next
    correlation = jnp.einsum('hrd,hsd->hrs', solution, key_all, precision=highest) * weights
    within = jnp.einsum('hrs,hse->hre', correlation, value_all, precision=highest)
    earlier = jnp.einsum('hrd,hed->hre', solution, memory, precision=highest)
    return carried[..., None] * earlier + within


def reference(queries, key_vectors, value_vectors, gate_bins, doc_lengths, decay_rates, ridge_terms):
    head_count = decay_rates.shape[0]
    key_width = key_vectors.shape[1] // head_count
    value_width = value_vectors.shape[1] // head_count
    block_count = INPUT_LENGTH // S_DEV
    doc_starts = (jnp.cumsum(doc_lengths, dtype=jnp.int32) - doc_lengths).astype(jnp.int32)
    element_offsets = jnp.arange(INPUT_LENGTH + 1, dtype=jnp.int32) - 1
    doc_all = jnp.sum((doc_starts[None, :] <= element_offsets[:, None]).astype(jnp.int32), axis=1, dtype=jnp.int32) - 1
    prior_docs = doc_all[:-1].reshape(block_count, S_DEV)[:, 0]
    doc_ids = doc_all[1:].reshape(block_count, S_DEV)
    log_gate = (-decay_rates[None, :] * gate_bins.astype(jnp.float32) / INPUT_LENGTH).reshape(block_count, S_DEV, head_count)

    def heads_first(array, width):
        return array.reshape(block_count, S_DEV, head_count, width).astype(jnp.float32).transpose(0, 2, 1, 3)

    query_all = heads_first(queries, key_width)
    key_all = heads_first(key_vectors, key_width)
    value_all = heads_first(value_vectors, value_width)

    def advance(state, inputs):
        gram_state, memory = state
        query_block, key_block, value_block, gate_block, doc_block, prior_doc = inputs
        cumulative = jnp.cumsum(gate_block, axis=0)
        query_pos = jnp.arange(S_DEV, dtype=jnp.int32)
        weights, carried = gate_weights(cumulative, doc_block, cumulative, doc_block, query_pos, prior_doc)
        output = solve_and_read(query_block, key_block, value_block, weights, carried, gram_state, memory, ridge_terms)
        end_weights = jnp.where((doc_block == doc_block[-1])[None, :], jnp.exp(cumulative[-1][:, None] - cumulative.T), 0.0)
        shard_decay = jnp.where(doc_block[-1] == prior_doc, jnp.exp(cumulative[-1]), 0.0)
        gram_sum = jnp.einsum('hsa,hsb->hab', key_block * end_weights[..., None], key_block, precision=highest)
        memory_sum = jnp.einsum('hsa,hsb->hab', value_block * end_weights[..., None], key_block, precision=highest)
        gram_state = shard_decay[:, None, None] * gram_state + gram_sum
        memory = shard_decay[:, None, None] * memory + memory_sum
        return (gram_state, memory), output

    start_state = (jnp.zeros((head_count, key_width, key_width), jnp.float32),
                   jnp.zeros((head_count, value_width, key_width), jnp.float32))
    unused, layer_results = lax.scan(advance, start_state, (query_all, key_all, value_all, log_gate, doc_ids, prior_docs))
    return layer_results.transpose(0, 2, 1, 3).reshape(INPUT_LENGTH, head_count * value_width).astype(jnp.bfloat16)
```

```python
import functools

import jax
import jax.numpy as jnp
from jax import lax
from jax.experimental import pallas as pl
from jax.experimental.pallas import tpu as pltpu
from jax.sharding import PartitionSpec as P

ITERS = 4
guard = 1e-06
f32 = jnp.float32
bf16 = jnp.bfloat16
PAD = 8


def dot_nn(a, b):
    return lax.dot_general(a, b, (((1,), (0,)), ((), ())), preferred_element_type=f32)


def dot_nt(a, b):
    return lax.dot_general(a, b, (((1,), (1,)), ((), ())), preferred_element_type=f32)


def dot_tn(a, b):
    return lax.dot_general(a, b, (((0,), (0,)), ((), ())), preferred_element_type=f32)


def split(x):
    high = x.astype(bf16)
    low = (x - high.astype(f32)).astype(bf16)
    return high, low


def doc_of(doc_ref, position):
    count = jnp.zeros_like(position)
    start = jnp.int32(0)
    for index in range(doc_ref.shape[0]):
        count = count + (start <= position).astype(jnp.int32)
        start = start + doc_ref[index]
    return count


def split_bins(bins):
    whole = bins.astype(f32)
    high = jnp.floor(whole * (1.0 / 128.0))
    low = whole - 128.0 * high
    return high.astype(bf16), low.astype(bf16)


def pick(columns, head):
    lane = lax.broadcasted_iota(jnp.int32, columns.shape, 1)
    return jnp.sum(jnp.where(lane == head, columns, 0.0), axis=1, keepdims=True)


def upper(size):
    row = lax.broadcasted_iota(jnp.int32, (size, size), 0)
    col = lax.broadcasted_iota(jnp.int32, (size, size), 1)
    return jnp.where(row <= col, 1.0, 0.0).astype(bf16)


def outer_sums(key, value, weight):
    high, low = split(key.astype(f32) * weight)
    width = key.shape[1]
    both = dot_tn(jnp.concatenate([key, value], 1), jnp.concatenate([high, low], 1))
    return both[:, :width] + both[:, width:]


def sums_kernel(where_ref, doc_ref, rate_ref, key_ref, value_ref, bins_ref, out_ref, *, total, heads, width):
    shard = key_ref.shape[0]
    first = where_ref[0] * shard
    core = where_ref[1]
    high, low = split_bins(bins_ref[...])
    step = upper(shard)
    cumulative = 128.0 * dot_tn(step, high) + dot_tn(step, low)
    last = cumulative[shard - 1 : shard, :]
    position = first + lax.broadcasted_iota(jnp.int32, (shard, 1), 0)
    live = doc_of(doc_ref, position) == doc_of(doc_ref, first + shard - 1)
    through = doc_of(doc_ref, first + shard - 1) == doc_of(doc_ref, first - 1)
    for i in range(heads):
        head = core * heads + i
        scale = rate_ref[head] * (-1.0 / total)
        to_end = pick(last - cumulative, head)
        weight = jnp.where(live, jnp.exp(scale * to_end), 0.0)
        cols = slice(i * width, (i + 1) * width)
        out_ref[i, : 2 * width, :] = outer_sums(key_ref[:, cols], value_ref[:, cols], weight)
        decay = jnp.where(through, jnp.exp(scale * pick(last, head)), 0.0)
        out_ref[i, 2 * width :, :] = jnp.broadcast_to(decay, (PAD, width))


def solve_kernel(
    where_ref, doc_ref, rate_ref, ridge_ref, query_ref, key_ref, value_ref, bins_ref, state_ref, *rest,
    total, heads, width, turn,
):
    out_ref, row_ref, weight_ref = rest[-3:]
    shard, rows = key_ref.shape[0], query_ref.shape[0]
    core = where_ref[1]
    group = lax.rem(core + turn, shard // rows)
    first = where_ref[0] * shard
    start = core * rows
    high, low = split_bins(bins_ref[...])
    step = upper(shard)
    cumulative = 128.0 * dot_tn(step, high) + dot_tn(step, low)
    row_ref[...] = 128.0 * dot_tn(high, step) + dot_tn(low, step)
    token = lax.broadcasted_iota(jnp.int32, (shard, 1), 0)
    before_doc = doc_of(doc_ref, first + start - 1)
    own_pos = first + start + lax.broadcasted_iota(jnp.int32, (rows, 1), 0)
    own_doc = doc_of(doc_ref, own_pos)
    key_pos = first + start + lax.broadcasted_iota(jnp.int32, (1, rows), 1)
    allowed = (key_pos <= own_pos) & (doc_of(doc_ref, key_pos) == own_doc)
    goes_on = own_doc == before_doc
    mid_live = (token < start) & (doc_of(doc_ref, first + token) == before_doc)
    mid_through = before_doc == doc_of(doc_ref, first - 1)
    own = pl.ds(pl.multiple_of(start, rows), rows)
    before = jnp.sum(
        jnp.where(token == start - 1, cumulative, 0.0), axis=0, keepdims=True
    )
    relative = cumulative - before
    for i in range(heads):
        head = group * heads + i
        scale = rate_ref[head] * (-1.0 / total)
        ridge = ridge_ref[head]
        cols = slice(i * width, (i + 1) * width)
        rel = pick(relative, head)
        mid_weight = jnp.where(mid_live, jnp.exp(scale * jnp.maximum(-rel, 0.0)), 0.0)
        mid = outer_sums(key_ref[:, cols], value_ref[:, cols], mid_weight)
        mid_decay = jnp.where(mid_through, jnp.exp(scale * pick(before, head)), 0.0)
        state = mid_decay * state_ref[i, : 2 * width, :] + mid
        gram_high, gram_low = split(state[:width])
        mem_high, mem_low = split(state[width:])
        none = jnp.zeros_like(gram_low)
        key = key_ref[own, cols]
        value = value_ref[own, cols]
        left = jnp.concatenate([key, gram_high, gram_low], 0)
        right = jnp.concatenate([key, gram_high, none], 0)
        system = jnp.concatenate([left, right], 1)
        key_two = jnp.concatenate([key, key], 0)
        row = row_ref[pl.ds(head, 1), own]
        own_cum = jnp.sum(
            jnp.where(
                lax.broadcasted_iota(jnp.int32, (rows, heads * (shard // rows)), 1) == head,
                row_ref_cols(cumulative, start, rows),
                0.0,
            ),
            axis=1,
            keepdims=True,
        )
        weight_ref[i] = jnp.where(allowed, jnp.exp(scale * jnp.maximum(own_cum - row, 0.0)), 0.0)
        carried = jnp.where(goes_on, jnp.exp(scale * (own_cum - pick(before, head))), 0.0)
        query = query_ref[:, cols]
        direction = query.astype(f32)
        residual = direction
        energy = jnp.sum(residual * residual, axis=1, keepdims=True)
        solution = None
        for iteration in range(ITERS):
            if iteration == 0:
                product = dot_nt(query, left)
            else:
                product = dot_nt(jnp.concatenate(split(direction), 1), system)
            plain = product[:, :rows]
            weighted = plain * weight_ref[i]
            earlier = carried * (product[:, rows : rows + width] + product[:, rows + width :])
            if iteration < ITERS - 1:
                within = dot_nn(jnp.concatenate(split(weighted), 1), key_two)
                applied = earlier + within + ridge * direction
                curvature = jnp.sum(direction * applied, axis=1, keepdims=True)
            else:
                curvature = jnp.sum(plain * weighted, axis=1, keepdims=True) + jnp.sum(
                    direction * (earlier + ridge * direction), axis=1, keepdims=True
                )
            stepsize = energy / (curvature + guard)
            if iteration == 0:
                solution = stepsize * direction
                reads = stepsize * weighted
            else:
                solution = solution + stepsize * direction
                reads = reads + stepsize * weighted
            if iteration < ITERS - 1:
                residual = residual - stepsize * applied
                energy_next = jnp.sum(residual * residual, axis=1, keepdims=True)
                direction = residual + (energy_next / (energy + guard)) * direction
                energy = energy_next
        memory = jnp.concatenate(
            [jnp.concatenate([mem_high, mem_low], 0), jnp.concatenate([mem_high, none], 0)], 1
        )
        from_state = dot_nt(jnp.concatenate(split(solution), 1), memory)
        from_chunk = dot_nn(jnp.concatenate(split(reads), 1), jnp.concatenate([value, value], 0))
        result = carried * (from_state[:, :width] + from_state[:, width:]) + from_chunk
        out_ref[:, cols] = result.astype(out_ref.dtype)


def row_ref_cols(cumulative, start, rows):
    count = cumulative.shape[0] // rows
    picked = cumulative[:rows]
    for index in range(1, count):
        picked = jnp.where(start == index * rows, cumulative[index * rows : (index + 1) * rows], picked)
    return picked


def per_device(queries, key_vectors, value_vectors, gate_bins, doc_lengths, decay_rates, ridge_terms):
    head_count = decay_rates.shape[0]
    shard = key_vectors.shape[0]
    rows = queries.shape[0]
    width = key_vectors.shape[1] // head_count
    seq = lax.axis_size("seq")
    cores = lax.axis_size("sub")
    heads = head_count // cores
    total = shard * seq
    where = jnp.stack([lax.axis_index("seq"), lax.axis_index("sub")]).astype(jnp.int32)

    smem = pl.BlockSpec(memory_space=pltpu.SMEM)
    payload_rows = 2 * width + PAD

    def group_block(turn):
        return lambda i, where_ref: (0, lax.rem(where_ref[1] + turn, cores))

    def whole(i, where_ref):
        return (0, 0)

    sums = pl.pallas_call(
        functools.partial(sums_kernel, total=total, heads=heads, width=width),
        grid_spec=pltpu.PrefetchScalarGridSpec(
            num_scalar_prefetch=1,
            grid=(1,),
            in_specs=[
                smem,
                smem,
                pl.BlockSpec((shard, heads * width), group_block(0)),
                pl.BlockSpec((shard, heads * width), group_block(0)),
                pl.BlockSpec((shard, head_count), whole),
            ],
            out_specs=pl.BlockSpec((heads, payload_rows, width), lambda i, where_ref: (0, 0, 0)),
        ),
        out_shape=jax.ShapeDtypeStruct((heads, payload_rows, width), f32),
        name="shard_sums",
    )(where, doc_lengths, decay_rates, key_vectors, value_vectors, gate_bins)

    def decay_of(payload):
        return payload[:, 2 * width : 2 * width + 1, :]

    prior = None
    covered = 0
    while covered < seq - 1:
        if prior is None:
            prior = lax.ppermute(sums, "seq", [(i, i + 1) for i in range(seq - 1)])
            covered = 1
        else:
            local = jnp.where(
                (jnp.arange(payload_rows) < 2 * width)[None, :, None], sums, 0.0
            )
            inclusive = local + decay_of(sums) * prior
            shift = covered + 1
            received = lax.ppermute(inclusive, "seq", [(i, i + shift) for i in range(seq - shift)])
            local = jnp.where(
                (jnp.arange(payload_rows) < 2 * width)[None, :, None], prior, 0.0
            )
            prior = local + decay_of(prior) * received
            covered = covered + shift
    swapped = lax.ppermute(prior, "sub", [(i, (i + 1) % cores) for i in range(cores)])

    def solve(turn, state, output):
        in_specs = [
            smem,
            smem,
            smem,
            pl.BlockSpec((rows, heads * width), group_block(turn)),
            pl.BlockSpec((shard, heads * width), group_block(turn)),
            pl.BlockSpec((shard, heads * width), group_block(turn)),
            pl.BlockSpec((shard, head_count), whole),
            pl.BlockSpec((heads, payload_rows, width), lambda i, where_ref: (0, 0, 0)),
        ]
        operands = [where, doc_lengths, decay_rates, ridge_terms, queries, key_vectors, value_vectors, gate_bins, state]
        aliases = {}
        if output is not None:
            in_specs.append(pl.BlockSpec(memory_space=pl.ANY))
            aliases = {len(operands): 0}
            operands.append(output)
        return pl.pallas_call(
            functools.partial(solve_kernel, total=total, heads=heads, width=width, turn=turn),
            grid_spec=pltpu.PrefetchScalarGridSpec(
                num_scalar_prefetch=1,
                grid=(1,),
                in_specs=in_specs,
                out_specs=pl.BlockSpec((rows, heads * width), group_block(turn)),
                scratch_shapes=[
                    pltpu.VMEM((head_count, shard), f32),
                    pltpu.VMEM((heads, rows, rows), f32),
                ],
            ),
            out_shape=jax.ShapeDtypeStruct((rows, head_count * width), bf16),
            input_output_aliases=aliases,
            name=f"solve_{turn}",
        )(*operands)

    output = None
    for turn in range(cores):
        output = solve(turn, prior if turn == 0 else swapped, output)
    return output


def solution(mesh):
    in_specs = (
        P(("rep", "seq", "sub"), "head"),
        P(("rep", "seq"), "head"),
        P(("rep", "seq"), "head"),
        P(("rep", "seq"), "head"),
        P("rep"),
        P("head"),
        P("head"),
    )
    out_specs = P(("rep", "seq", "sub"), "head")
    return jax.shard_map(per_device, mesh=mesh, in_specs=in_specs, out_specs=out_specs, check_vma=False)
```

```python
import functools

import jax
import jax.numpy as jnp
from jax import lax
from jax.experimental import pallas as pl
from jax.experimental.pallas import tpu as pltpu
from jax.sharding import PartitionSpec as P

ITERS = 4
guard = 1e-06
f32 = jnp.float32
bf16 = jnp.bfloat16
PAD = 8
PER_STEP = 2


def dot_nn(a, b):
    return lax.dot_general(a, b, (((1,), (0,)), ((), ())), preferred_element_type=f32)


def dot_nt(a, b):
    return lax.dot_general(a, b, (((1,), (1,)), ((), ())), preferred_element_type=f32)


def split(x):
    high = x.astype(bf16)
    low = (x - high.astype(f32)).astype(bf16)
    return high, low


def iota(shape, axis):
    return lax.broadcasted_iota(jnp.int32, shape, axis)


def doc_of(doc_ref, position):
    count = jnp.zeros_like(position)
    start = jnp.int32(0)
    for index in range(doc_ref.shape[0]):
        count = count + (start <= position).astype(jnp.int32)
        start = start + doc_ref[index]
    return count


def split_bins(bins):
    whole = bins.astype(f32)
    high = jnp.floor(whole * (1.0 / 128.0))
    low = whole - 128.0 * high
    return high.astype(bf16), low.astype(bf16)


def running_rows(bins):
    size = bins.shape[1]
    high, low = split_bins(bins)
    step = jnp.where(iota((size, size), 0) <= iota((size, size), 1), 1.0, 0.0).astype(bf16)
    return 128.0 * dot_nn(high, step) + dot_nn(low, step)


def running_columns(bins):
    size = bins.shape[1]
    high, low = split_bins(bins)
    step = jnp.where(iota((size, size), 1) <= iota((size, size), 0), 1.0, 0.0).astype(bf16)
    return 128.0 * dot_nt(step, high) + dot_nt(step, low)


def scale_column(rate_ref, total):
    count = rate_ref.shape[0]
    column = jnp.zeros((count, 1), f32)
    for head in range(count):
        column = jnp.where(iota((count, 1), 0) == head, rate_ref[head], column)
    return column * (-1.0 / total)


def weighted_sums(key_t, weight, both):
    width = key_t.shape[0]
    product = dot_nn(jnp.concatenate(split(key_t.astype(f32) * weight), 0), both)
    return product[:width] + product[width:]


def pack_gram(gram, decay):
    width = gram.shape[0]
    half = width // 2
    turned = pltpu.roll(gram[half:], half, 1)
    row, col = iota((half, width), 0), iota((half, width), 1)
    packed = jnp.where((col < half) & (row > col), turned, gram[:half])
    diagonal = jnp.sum(jnp.where(row == col, turned, 0.0), axis=0, keepdims=True)
    tail = jnp.where(iota((PAD, width), 0) == 0, diagonal, decay)
    return packed, tail


def unpack_gram(packed, diagonal):
    half, width = packed.shape
    turned = pltpu.roll(packed, half, 1)
    crossed = jnp.concatenate([packed, turned], 0).T
    row, col = iota((half, width), 0), iota((half, width), 1)
    top = jnp.where(row <= col, packed, crossed[:half])
    low_col = col - half
    bottom = jnp.where((low_col >= 0) & (row > low_col), turned, crossed[half:])
    bottom = jnp.where(row == low_col, pltpu.roll(jnp.broadcast_to(diagonal, (half, width)), half, 1), bottom)
    return jnp.concatenate([top, bottom], 0)


def sums_kernel(
    where_ref, doc_ref, rate_ref, key_ref, value_ref, bins_ref, gram_ref, memory_ref, weight_ref, decay_ref,
    *, total, heads, width,
):
    shard = key_ref.shape[0]
    first = where_ref[0] * shard
    core = where_ref[1]
    scale = scale_column(rate_ref, total)
    cumulative = running_rows(bins_ref[...])
    last = cumulative[:, shard - 1 :]
    position = first + iota((1, shard), 1)
    end_doc = doc_of(doc_ref, first + shard - 1)
    weight_ref[...] = jnp.where(
        doc_of(doc_ref, position) == end_doc, jnp.exp(scale * (last - cumulative)), 0.0
    )
    through = end_doc == doc_of(doc_ref, first - 1)
    decay_ref[...] = jnp.broadcast_to(jnp.where(through, jnp.exp(scale * last), 0.0), decay_ref.shape)
    for i in range(heads):
        head = core * heads + i
        cols = slice(i * width, (i + 1) * width)
        key = key_ref[:, cols]
        both = jnp.concatenate([key, value_ref[:, cols]], 1)
        sums = weighted_sums(key.T, weight_ref[pl.ds(head, 1), :], both)
        packed, tail = pack_gram(sums[:, :width], decay_ref[pl.ds(head, 1), :])
        gram_ref[i, : width // 2, :] = packed
        gram_ref[i, width // 2 :, :] = tail
        memory_ref[i] = sums[:, width:]


def prepare_kernel(
    where_ref, doc_ref, rate_ref, query_ref, key_ref, value_ref, bins_ref,
    gate_ref, query_t_ref, key_t_ref, value_t_ref, within_ref, mid_gram_ref, mid_memory_ref, carried_ref,
    row_ref, column_ref, mid_ref, decay_ref, *, total, width,
):
    shard, rows = key_ref.shape[0], query_ref.shape[0]
    first = where_ref[0] * shard
    start = where_ref[1] * rows
    own = pl.ds(pl.multiple_of(start, rows), rows)
    before_doc = doc_of(doc_ref, first + start - 1)
    key_pos = first + start + iota((rows, 1), 0)
    own_pos = first + start + iota((1, rows), 1)
    own_doc = doc_of(doc_ref, own_pos)

    @pl.when(pl.program_id(0) == 0)
    def _():
        scale = scale_column(rate_ref, total)
        bins = bins_ref[...]
        cumulative = running_rows(bins)
        row_ref[...] = cumulative
        column_ref[...] = running_columns(bins)
        token = iota((1, shard), 1)
        before = jnp.sum(jnp.where(token == start - 1, cumulative, 0.0), axis=1, keepdims=True)
        mid_live = (token < start) & (doc_of(doc_ref, first + token) == before_doc)
        mid_ref[...] = jnp.where(
            mid_live, jnp.exp(scale * jnp.maximum(before - cumulative, 0.0)), 0.0
        )
        through = before_doc == doc_of(doc_ref, first - 1)
        decay_ref[...] = jnp.broadcast_to(
            jnp.where(through, jnp.exp(scale * before), 0.0), decay_ref.shape
        )
        carried_ref[...] = jnp.where(
            own_doc == before_doc, jnp.exp(scale * jnp.maximum(row_ref[:, own] - before, 0.0)), 0.0
        )

    allowed = (key_pos <= own_pos) & (doc_of(doc_ref, key_pos) == own_doc)
    columns = column_ref[own, :]
    for i in range(query_ref.shape[1] // width):
        head = pl.program_id(0) * PER_STEP + i
        scale = rate_ref[head] * (-1.0 / total)
        cols = slice(i * width, (i + 1) * width)
        key_t = key_ref[:, cols].T
        both = jnp.concatenate([key_ref[:, cols], value_ref[:, cols]], 1)
        sums = weighted_sums(key_t, mid_ref[pl.ds(head, 1), :], both)
        packed, tail = pack_gram(sums[:, :width], decay_ref[pl.ds(head, 1), :])
        mid_gram_ref[i, : width // 2, :] = packed
        mid_gram_ref[i, width // 2 :, :] = tail
        mid_memory_ref[i] = sums[:, width:]
        key_own = key_ref[own, cols]
        own_t = key_own.T
        query_t = query_ref[:, cols].T
        query_t_ref[i] = query_t
        key_t_ref[i] = own_t
        value_t_ref[i] = value_ref[own, cols].T
        column = jnp.sum(jnp.where(iota(columns.shape, 1) == head, columns, 0.0), axis=1, keepdims=True)
        gap = jnp.maximum(row_ref[pl.ds(head, 1), own] - column, 0.0)
        gate = jnp.where(allowed, jnp.exp(scale * gap), 0.0)
        gate_ref[i] = gate
        weighted = dot_nn(key_own, query_t) * gate
        within_ref[i] = dot_nn(jnp.concatenate([own_t, own_t], 1), jnp.concatenate(split(weighted), 0))


def solve_kernel(
    where_ref, ridge_ref, key_ref, gate_ref, query_t_ref, key_t_ref, value_t_ref, within_ref, mid_ref, carried_ref,
    gram_ref, solution_ref, chunk_ref, *, cores, turn, width,
):
    rows = query_t_ref.shape[2]
    core = where_ref[1]
    steps = pl.num_programs(0)
    group = lax.rem(core + turn, cores)
    own = pl.ds(pl.multiple_of(core * rows, rows), rows)
    half = width // 2
    per_step = range(query_t_ref.shape[0])
    base = (group * steps + pl.program_id(0)) * query_t_ref.shape[0]

    def row_sum(x):
        return jnp.sum(x, axis=0, keepdims=True)

    ridge = [ridge_ref[base + i] for i in per_step]
    carried = [carried_ref[pl.ds(base + i, 1), :] for i in per_step]
    system, keys, key_pair = [], [], []
    direction, residual, energy, result = [], [], [], []
    for i in per_step:
        cols = slice(i * width, (i + 1) * width)
        decay = mid_ref[i, half + 1 : half + 2, :]
        packed = mid_ref[i, :half, :] + decay * gram_ref[i, :half, :]
        diagonal = mid_ref[i, half : half + 1, :] + decay * gram_ref[i, half : half + 1, :]
        high, low = split(unpack_gram(packed, diagonal))
        key = key_ref[own, cols]
        keys.append(jnp.concatenate([key, key], 1))
        key_pair.append(jnp.concatenate([key_t_ref[i], key_t_ref[i]], 1))
        system.append(
            jnp.concatenate(
                [jnp.concatenate([high, low], 0), jnp.concatenate([high, jnp.zeros_like(low)], 0)], 1
            )
        )
        direction.append(query_t_ref[i].astype(f32))
        residual.append(direction[i])
        energy.append(row_sum(direction[i] * direction[i]))
        result.append(None)
    for iteration in range(ITERS):
        last = iteration == ITERS - 1
        earlier = []
        parts = []
        for i in per_step:
            if iteration == 0:
                product = dot_nn(system[i][:, :width], query_t_ref[i])
            else:
                pair = jnp.concatenate(split(direction[i]), 0)
                product = dot_nn(system[i], pair)
                plain = dot_nn(keys[i], pair)
                parts.append((plain, plain * gate_ref[i]))
            earlier.append(
                carried[i] * (product[:width] + product[width:]) + ridge[i] * direction[i]
            )
        for i in per_step:
            if iteration == 0:
                applied = earlier[i] + within_ref[i]
                curvature = row_sum(direction[i] * applied)
            elif not last:
                applied = earlier[i] + dot_nn(key_pair[i], jnp.concatenate(split(parts[i][1]), 0))
                curvature = row_sum(direction[i] * applied)
            else:
                curvature = row_sum(parts[i][0] * parts[i][1]) + row_sum(direction[i] * earlier[i])
            stepsize = energy[i] / (curvature + guard)
            moved = stepsize * direction[i]
            result[i] = moved if iteration == 0 else result[i] + moved
            if not last:
                residual[i] = residual[i] - stepsize * applied
                energy_next = row_sum(residual[i] * residual[i])
                direction[i] = residual[i] + (energy_next / (energy[i] + guard)) * direction[i]
                energy[i] = energy_next
    for i in per_step:
        weighted = dot_nn(keys[i], jnp.concatenate(split(result[i]), 0)) * gate_ref[i]
        value_t = value_t_ref[i]
        chunk = dot_nn(jnp.concatenate([value_t, value_t], 1), jnp.concatenate(split(weighted), 0))
        chunk_ref[i] = chunk.T
        high, low = split(carried[i] * result[i])
        solution_ref[i] = jnp.concatenate([high.T, low.T], 1)


def read_kernel(where_ref, solution_ref, chunk_ref, mid_ref, mid_memory_ref, memory_ref, *rest, width):
    out_ref = rest[-1]
    half = width // 2
    for i in range(solution_ref.shape[0]):
        decay = mid_ref[i, 1:2, :]
        memory = mid_memory_ref[i] + decay * memory_ref[i]
        high, low = split(memory)
        pair = jnp.concatenate(
            [jnp.concatenate([high, high], 0), jnp.concatenate([low, jnp.zeros_like(low)], 0)], 1
        )
        product = dot_nn(solution_ref[i], pair)
        out = product[:, :width] + product[:, width:] + chunk_ref[i]
        out_ref[:, i * width : (i + 1) * width] = out.astype(out_ref.dtype)


def per_device(queries, key_vectors, value_vectors, gate_bins, doc_lengths, decay_rates, ridge_terms):
    head_count = decay_rates.shape[0]
    shard = key_vectors.shape[0]
    rows = queries.shape[0]
    width = key_vectors.shape[1] // head_count
    half = width // 2
    seq = lax.axis_size("seq")
    cores = lax.axis_size("sub")
    heads = head_count // cores
    total = shard * seq
    where = jnp.stack([lax.axis_index("seq"), lax.axis_index("sub")]).astype(jnp.int32)
    bins = gate_bins.T
    smem = pl.BlockSpec(memory_space=pltpu.SMEM)
    any_space = pl.BlockSpec(memory_space=pl.ANY)

    def full(*shape):
        return pl.BlockSpec(shape, lambda i, where_ref: (0,) * len(shape))

    def call(kernel, grid, in_specs, out_specs, out_shape, scratch, name, cost, **options):
        return pl.pallas_call(
            kernel,
            grid_spec=pltpu.PrefetchScalarGridSpec(
                num_scalar_prefetch=1,
                grid=(grid,),
                in_specs=in_specs,
                out_specs=out_specs,
                scratch_shapes=scratch,
            ),
            out_shape=out_shape,
            name=name,
            cost_estimate=pl.CostEstimate(flops=cost, bytes_accessed=4 << 20, transcendentals=0),
            **options,
        )

    group = pl.BlockSpec((shard, heads * width), lambda i, where_ref: (0, where_ref[1]))
    gram_sum, memory_sum = call(
        functools.partial(sums_kernel, total=total, heads=heads, width=width),
        1,
        [smem, smem, group, group, full(head_count, shard)],
        [full(heads, half + PAD, width), full(heads, width, width)],
        [
            jax.ShapeDtypeStruct((heads, half + PAD, width), f32),
            jax.ShapeDtypeStruct((heads, width, width), f32),
        ],
        [pltpu.VMEM((head_count, shard), f32), pltpu.VMEM((head_count, width), f32)],
        "shard_sums",
        1 << 30,
    )(where, doc_lengths, decay_rates, key_vectors, value_vectors, bins)

    step = min(PER_STEP, heads)

    def head_block(*shape):
        return pl.BlockSpec((step, *shape), lambda i, where_ref: (i,) + (0,) * len(shape))

    def step_block(count):
        return pl.BlockSpec((count, step * width), lambda i, where_ref: (0, i))

    def per_head(*shape, dtype=f32):
        return jax.ShapeDtypeStruct((head_count, *shape), dtype)

    gate, query_t, key_t, value_t, within, mid_gram, mid_memory, carried = call(
        functools.partial(prepare_kernel, total=total, width=width),
        head_count // step,
        [smem, smem, step_block(rows), step_block(shard), step_block(shard), full(head_count, shard)],
        [
            head_block(rows, rows),
            head_block(width, rows),
            head_block(width, rows),
            head_block(width, rows),
            head_block(width, rows),
            head_block(half + PAD, width),
            head_block(width, width),
            full(head_count, rows),
        ],
        [
            per_head(rows, rows),
            per_head(width, rows, dtype=bf16),
            per_head(width, rows, dtype=bf16),
            per_head(width, rows, dtype=bf16),
            per_head(width, rows),
            per_head(half + PAD, width),
            per_head(width, width),
            per_head(rows),
        ],
        [
            pltpu.VMEM((head_count, shard), f32),
            pltpu.VMEM((shard, head_count), f32),
            pltpu.VMEM((head_count, shard), f32),
            pltpu.VMEM((head_count, width), f32),
        ],
        "prepare",
        4 << 30,
    )(where, doc_lengths, decay_rates, queries, key_vectors, value_vectors, bins)

    own_decay = gram_sum[:, half + 1 : half + 2, :]
    body = (jnp.arange(half + PAD) < half + 1)[None, :, None]
    gram_prior = memory_prior = None
    covered = 0
    while covered < seq - 1:
        if covered == 0:
            hop = functools.partial(lax.ppermute, axis_name="seq", perm=[(i, i + 1) for i in range(seq - 1)])
            gram_prior, memory_prior = hop(gram_sum), hop(memory_sum)
            covered = 1
        else:
            shift = covered + 1
            hop = functools.partial(
                lax.ppermute, axis_name="seq", perm=[(i, i + shift) for i in range(seq - shift)]
            )
            prior_decay = gram_prior[:, half + 1 : half + 2, :]
            gram_in = hop(jnp.where(body, gram_sum, 0.0) + own_decay * gram_prior)
            memory_in = hop(memory_sum + own_decay * memory_prior)
            gram_prior = jnp.where(body, gram_prior, 0.0) + prior_decay * gram_in
            memory_prior = memory_prior + prior_decay * memory_in
            covered = covered + shift

    def swap(x):
        return lax.ppermute(x, "sub", [(i, (i + 1) % cores) for i in range(cores)])

    steps = heads // step
    solved = []
    for turn in range(cores):

        def group_index(i, where_ref, turn=turn):
            return lax.rem(where_ref[1] + turn, cores) * steps + i

        def block(*shape):
            return pl.BlockSpec(
                (step, *shape), lambda i, where_ref: (group_index(i, where_ref),) + (0,) * len(shape)
            )

        def local_block(*shape):
            return pl.BlockSpec((step, *shape), lambda i, where_ref: (i,) + (0,) * len(shape))

        solved.append(
            call(
                functools.partial(solve_kernel, cores=cores, turn=turn, width=width),
                steps,
                [
                    smem,
                    pl.BlockSpec((shard, step * width), lambda i, where_ref: (0, group_index(i, where_ref))),
                    block(rows, rows),
                    block(width, rows),
                    block(width, rows),
                    block(width, rows),
                    block(width, rows),
                    block(half + PAD, width),
                    full(head_count, rows),
                    local_block(half + PAD, width),
                ],
                [local_block(rows, 2 * width), local_block(rows, width)],
                [
                    jax.ShapeDtypeStruct((heads, rows, 2 * width), bf16),
                    jax.ShapeDtypeStruct((heads, rows, width), f32),
                ],
                [],
                f"solve_{turn}",
                2 << 30,
            )(
                where, ridge_terms, key_vectors, gate, query_t, key_t, value_t, within, mid_gram, carried,
                gram_prior if turn == 0 else swap(gram_prior),
            )
        )

    output = None
    for turn in range(cores):

        def group_all(*shape, turn=turn):
            return pl.BlockSpec(
                (heads, *shape),
                lambda i, where_ref: (lax.rem(where_ref[1] + turn, cores),) + (0,) * len(shape),
            )

        in_specs = [
            full(heads, rows, 2 * width),
            full(heads, rows, width),
            pl.BlockSpec(
                (heads, PAD, width),
                lambda i, where_ref, turn=turn: (lax.rem(where_ref[1] + turn, cores), half // PAD, 0),
            ),
            group_all(width, width),
            full(heads, width, width),
        ]
        operands = [where, *solved[turn], mid_gram, mid_memory, memory_prior if turn == 0 else swap(memory_prior)]
        aliases = {}
        if output is not None:
            aliases = {len(operands): 0}
            in_specs.append(any_space)
            operands.append(output)
        output = call(
            functools.partial(read_kernel, width=width),
            1,
            in_specs,
            pl.BlockSpec(
                (rows, heads * width), lambda i, where_ref, turn=turn: (0, lax.rem(where_ref[1] + turn, cores))
            ),
            jax.ShapeDtypeStruct((rows, head_count * width), bf16),
            [],
            f"read_{turn}",
            1 << 28,
            input_output_aliases=aliases,
        )(*operands)
    return output


def solution(mesh):
    in_specs = (
        P(("rep", "seq", "sub"), "head"),
        P(("rep", "seq"), "head"),
        P(("rep", "seq"), "head"),
        P(("rep", "seq"), "head"),
        P("rep"),
        P("head"),
        P("head"),
    )
    out_specs = P(("rep", "seq", "sub"), "head")
    return jax.shard_map(per_device, mesh=mesh, in_specs=in_specs, out_specs=out_specs, check_vma=False)
```

```python
import functools

import jax
import jax.numpy as jnp
from jax import lax
from jax.experimental import pallas as pl
from jax.experimental.pallas import tpu as pltpu
from jax.sharding import PartitionSpec as P

ITERS = 4
guard = 1e-06
f32 = jnp.float32
bf16 = jnp.bfloat16
PAD = 8
PER_STEP = 4
VMEM = 24 << 20


def dot_nn(a, b):
    return lax.dot_general(a, b, (((1,), (0,)), ((), ())), preferred_element_type=f32)


def dot_nt(a, b):
    return lax.dot_general(a, b, (((1,), (1,)), ((), ())), preferred_element_type=f32)


def split(x):
    high = x.astype(bf16)
    low = (x - high.astype(f32)).astype(bf16)
    return high, low


def iota(shape, axis):
    return lax.broadcasted_iota(jnp.int32, shape, axis)


def doc_of(doc_ref, position):
    count = jnp.zeros_like(position)
    start = jnp.int32(0)
    for index in range(doc_ref.shape[0]):
        count = count + (start <= position).astype(jnp.int32)
        start = start + doc_ref[index]
    return count


def split_bins(bins):
    whole = bins.astype(f32)
    high = jnp.floor(whole * (1.0 / 128.0))
    low = whole - 128.0 * high
    return high.astype(bf16), low.astype(bf16)


def running_rows(bins):
    size = bins.shape[1]
    high, low = split_bins(bins)
    step = jnp.where(iota((size, size), 0) <= iota((size, size), 1), 1.0, 0.0).astype(bf16)
    return 128.0 * dot_nn(high, step) + dot_nn(low, step)


def running_columns(bins):
    size = bins.shape[1]
    high, low = split_bins(bins)
    step = jnp.where(iota((size, size), 1) <= iota((size, size), 0), 1.0, 0.0).astype(bf16)
    return 128.0 * dot_nt(step, high) + dot_nt(step, low)


def scale_column(rate_ref, total):
    count = rate_ref.shape[0]
    column = jnp.zeros((count, 1), f32)
    for head in range(count):
        column = jnp.where(iota((count, 1), 0) == head, rate_ref[head], column)
    return column * (-1.0 / total)


def weighted_sums(key_t, weight, both):
    width = key_t.shape[0]
    product = dot_nn(jnp.concatenate(split(key_t.astype(f32) * weight), 0), both)
    return product[:width] + product[width:]


def pack_gram(gram, decay):
    width = gram.shape[0]
    half = width // 2
    turned = pltpu.roll(gram[half:], half, 1)
    row, col = iota((half, width), 0), iota((half, width), 1)
    packed = jnp.where((col < half) & (row > col), turned, gram[:half])
    diagonal = jnp.sum(jnp.where(row == col, turned, 0.0), axis=0, keepdims=True)
    tail = jnp.where(iota((PAD, width), 0) == 0, diagonal, decay)
    return packed, tail


def unpack_gram(packed, diagonal):
    half, width = packed.shape
    turned = pltpu.roll(packed, half, 1)
    crossed = jnp.concatenate([packed, turned], 0).T
    row, col = iota((half, width), 0), iota((half, width), 1)
    top = jnp.where(row <= col, packed, crossed[:half])
    low_col = col - half
    bottom = jnp.where((low_col >= 0) & (row > low_col), turned, crossed[half:])
    bottom = jnp.where(row == low_col, pltpu.roll(jnp.broadcast_to(diagonal, (half, width)), half, 1), bottom)
    return jnp.concatenate([top, bottom], 0)


def sums_kernel(
    where_ref, doc_ref, rate_ref, key_ref, value_ref, bins_ref, gram_ref, memory_ref, weight_ref, decay_ref,
    *, total, heads, width,
):
    shard = key_ref.shape[0]
    first = where_ref[0] * shard
    core = where_ref[1]
    scale = scale_column(rate_ref, total)
    cumulative = running_rows(bins_ref[...])
    last = cumulative[:, shard - 1 :]
    position = first + iota((1, shard), 1)
    end_doc = doc_of(doc_ref, first + shard - 1)
    weight_ref[...] = jnp.where(
        doc_of(doc_ref, position) == end_doc, jnp.exp(scale * (last - cumulative)), 0.0
    )
    through = end_doc == doc_of(doc_ref, first - 1)
    decay_ref[...] = jnp.broadcast_to(jnp.where(through, jnp.exp(scale * last), 0.0), decay_ref.shape)
    for i in range(heads):
        head = core * heads + i
        cols = slice(i * width, (i + 1) * width)
        key = key_ref[:, cols]
        both = jnp.concatenate([key, value_ref[:, cols]], 1)
        sums = weighted_sums(key.T, weight_ref[pl.ds(head, 1), :], both)
        packed, tail = pack_gram(sums[:, :width], decay_ref[pl.ds(head, 1), :])
        gram_ref[i, : width // 2, :] = packed
        gram_ref[i, width // 2 :, :] = tail
        memory_ref[i] = sums[:, width:]


def prepare_kernel(
    where_ref, doc_ref, rate_ref, query_ref, key_ref, value_ref, bins_ref,
    gate_ref, query_t_ref, key_t_ref, value_t_ref, within_ref, mid_gram_ref, mid_memory_ref, carried_ref,
    row_ref, column_ref, mid_ref, decay_ref, *, total, width,
):
    shard, rows = key_ref.shape[0], query_ref.shape[0]
    first = where_ref[0] * shard
    start = where_ref[1] * rows
    own = pl.ds(pl.multiple_of(start, rows), rows)
    before_doc = doc_of(doc_ref, first + start - 1)
    key_pos = first + start + iota((rows, 1), 0)
    own_pos = first + start + iota((1, rows), 1)
    own_doc = doc_of(doc_ref, own_pos)

    @pl.when(pl.program_id(0) == 0)
    def _():
        scale = scale_column(rate_ref, total)
        bins = bins_ref[...]
        cumulative = running_rows(bins)
        row_ref[...] = cumulative
        column_ref[...] = running_columns(bins)
        token = iota((1, shard), 1)
        before = jnp.sum(jnp.where(token == start - 1, cumulative, 0.0), axis=1, keepdims=True)
        mid_live = (token < start) & (doc_of(doc_ref, first + token) == before_doc)
        mid_ref[...] = jnp.where(
            mid_live, jnp.exp(scale * jnp.maximum(before - cumulative, 0.0)), 0.0
        )
        through = before_doc == doc_of(doc_ref, first - 1)
        decay_ref[...] = jnp.broadcast_to(
            jnp.where(through, jnp.exp(scale * before), 0.0), decay_ref.shape
        )
        carried_ref[...] = jnp.where(
            own_doc == before_doc, jnp.exp(scale * jnp.maximum(row_ref[:, own] - before, 0.0)), 0.0
        )

    allowed = (key_pos <= own_pos) & (doc_of(doc_ref, key_pos) == own_doc)
    columns = column_ref[own, :]
    for i in range(query_ref.shape[1] // width):
        head = pl.program_id(0) * PER_STEP + i
        scale = rate_ref[head] * (-1.0 / total)
        cols = slice(i * width, (i + 1) * width)
        key_t = key_ref[:, cols].T
        both = jnp.concatenate([key_ref[:, cols], value_ref[:, cols]], 1)
        sums = weighted_sums(key_t, mid_ref[pl.ds(head, 1), :], both)
        packed, tail = pack_gram(sums[:, :width], decay_ref[pl.ds(head, 1), :])
        mid_gram_ref[i, : width // 2, :] = packed
        mid_gram_ref[i, width // 2 :, :] = tail
        mid_memory_ref[i] = sums[:, width:]
        key_own = key_ref[own, cols]
        own_t = key_own.T
        query_t = query_ref[:, cols].T
        query_t_ref[i] = query_t
        key_t_ref[i] = own_t
        value_t_ref[i] = value_ref[own, cols].T
        column = jnp.sum(jnp.where(iota(columns.shape, 1) == head, columns, 0.0), axis=1, keepdims=True)
        gap = jnp.maximum(row_ref[pl.ds(head, 1), own] - column, 0.0)
        gate = jnp.where(allowed, jnp.exp(scale * gap), 0.0)
        gate_ref[i] = gate
        weighted = dot_nn(key_own, query_t) * gate
        within_ref[i] = dot_nn(jnp.concatenate([own_t, own_t], 1), jnp.concatenate(split(weighted), 0))


def solve_kernel(
    where_ref, ridge_ref, key_ref, gate_ref, query_t_ref, key_t_ref, value_t_ref, within_ref, mid_ref, carried_ref,
    gram_ref, solution_ref, chunk_ref, *, cores, turn, width,
):
    rows = query_t_ref.shape[2]
    core = where_ref[1]
    steps = pl.num_programs(0)
    group = lax.rem(core + turn, cores)
    own = pl.ds(pl.multiple_of(core * rows, rows), rows)
    half = width // 2
    per_step = range(query_t_ref.shape[0])
    base = (group * steps + pl.program_id(0)) * query_t_ref.shape[0]

    def row_sum(x):
        return jnp.sum(x, axis=0, keepdims=True)

    def head_program(i):
        cols = slice(i * width, (i + 1) * width)
        ridge = ridge_ref[base + i]
        carried = carried_ref[pl.ds(base + i, 1), :]
        decay = mid_ref[i, half + 1 : half + 2, :]
        packed = mid_ref[i, :half, :] + decay * gram_ref[i, :half, :]
        diagonal = mid_ref[i, half : half + 1, :] + decay * gram_ref[i, half : half + 1, :]
        high, low = split(unpack_gram(packed, diagonal))
        system = jnp.concatenate(
            [jnp.concatenate([high, low], 0), jnp.concatenate([high, jnp.zeros_like(low)], 0)], 1
        )
        key = key_ref[own, cols]
        keys = jnp.concatenate([key, key], 1)
        key_pair = jnp.concatenate([key_t_ref[i], key_t_ref[i]], 1)
        query_t = query_t_ref[i]
        direction = query_t.astype(f32)
        residual = direction
        energy = row_sum(direction * direction)
        result = None
        yield
        for iteration in range(ITERS):
            last = iteration == ITERS - 1
            if iteration == 0:
                product = dot_nn(system[:, :width], query_t)
            else:
                pair = jnp.concatenate(split(direction), 0)
                plain = dot_nn(keys, pair)
                product = dot_nn(system, pair)
            yield
            if iteration > 0:
                weighted = plain * gate_ref[i]
                if not last:
                    weighted_pair = jnp.concatenate(split(weighted), 0)
            earlier = carried * (product[:width] + product[width:]) + ridge * direction
            yield
            if iteration == 0:
                applied = earlier + within_ref[i]
            elif not last:
                within = dot_nn(key_pair, weighted_pair)
                yield
                applied = earlier + within
            if last:
                curvature = row_sum(plain * weighted) + row_sum(direction * earlier)
            else:
                curvature = row_sum(direction * applied)
            stepsize = energy / (curvature + guard)
            moved = stepsize * direction
            result = moved if iteration == 0 else result + moved
            if not last:
                residual = residual - stepsize * applied
                energy_next = row_sum(residual * residual)
                direction = residual + (energy_next / (energy + guard)) * direction
                energy = energy_next
            yield
        plain = dot_nn(keys, jnp.concatenate(split(result), 0))
        high, low = split(carried * result)
        solution_ref[i] = jnp.concatenate([high.T, low.T], 1)
        yield
        weighted_pair = jnp.concatenate(split(plain * gate_ref[i]), 0)
        yield
        value_t = value_t_ref[i]
        chunk = dot_nn(jnp.concatenate([value_t, value_t], 1), weighted_pair)
        yield
        chunk_ref[i] = chunk.T

    programs = [head_program(i) for i in per_step]
    running = []
    while programs or running:
        if programs:
            running.append(programs.pop(0))
        for program in list(running):
            if next(program, running) is running:
                running.remove(program)


def read_kernel(where_ref, solution_ref, chunk_ref, mid_ref, mid_memory_ref, memory_ref, *rest, width):
    out_ref = rest[-1]
    half = width // 2
    for i in range(solution_ref.shape[0]):
        decay = mid_ref[i, 1:2, :]
        memory = mid_memory_ref[i] + decay * memory_ref[i]
        high, low = split(memory)
        pair = jnp.concatenate(
            [jnp.concatenate([high, high], 0), jnp.concatenate([low, jnp.zeros_like(low)], 0)], 1
        )
        product = dot_nn(solution_ref[i], pair)
        out = product[:, :width] + product[:, width:] + chunk_ref[i]
        out_ref[:, i * width : (i + 1) * width] = out.astype(out_ref.dtype)


def per_device(queries, key_vectors, value_vectors, gate_bins, doc_lengths, decay_rates, ridge_terms):
    head_count = decay_rates.shape[0]
    shard = key_vectors.shape[0]
    rows = queries.shape[0]
    width = key_vectors.shape[1] // head_count
    half = width // 2
    seq = lax.axis_size("seq")
    cores = lax.axis_size("sub")
    heads = head_count // cores
    total = shard * seq
    where = jnp.stack([lax.axis_index("seq"), lax.axis_index("sub")]).astype(jnp.int32)
    bins = gate_bins.T
    smem = pl.BlockSpec(memory_space=pltpu.SMEM)
    any_space = pl.BlockSpec(memory_space=pl.ANY)

    def full(*shape):
        return pl.BlockSpec(shape, lambda i, where_ref: (0,) * len(shape))

    def call(kernel, grid, in_specs, out_specs, out_shape, scratch, name, cost, **options):
        return pl.pallas_call(
            kernel,
            grid_spec=pltpu.PrefetchScalarGridSpec(
                num_scalar_prefetch=1,
                grid=(grid,),
                in_specs=in_specs,
                out_specs=out_specs,
                scratch_shapes=scratch,
            ),
            out_shape=out_shape,
            name=name,
            cost_estimate=pl.CostEstimate(flops=cost, bytes_accessed=4 << 20, transcendentals=0),
            compiler_params=pltpu.CompilerParams(vmem_limit_bytes=VMEM),
            **options,
        )

    group = pl.BlockSpec((shard, heads * width), lambda i, where_ref: (0, where_ref[1]))
    gram_sum, memory_sum = call(
        functools.partial(sums_kernel, total=total, heads=heads, width=width),
        1,
        [smem, smem, group, group, full(head_count, shard)],
        [full(heads, half + PAD, width), full(heads, width, width)],
        [
            jax.ShapeDtypeStruct((heads, half + PAD, width), f32),
            jax.ShapeDtypeStruct((heads, width, width), f32),
        ],
        [pltpu.VMEM((head_count, shard), f32), pltpu.VMEM((head_count, width), f32)],
        "shard_sums",
        1 << 30,
    )(where, doc_lengths, decay_rates, key_vectors, value_vectors, bins)

    step = min(PER_STEP, heads)

    def head_block(*shape):
        return pl.BlockSpec((step, *shape), lambda i, where_ref: (i,) + (0,) * len(shape))

    def step_block(count):
        return pl.BlockSpec((count, step * width), lambda i, where_ref: (0, i))

    def per_head(*shape, dtype=f32):
        return jax.ShapeDtypeStruct((head_count, *shape), dtype)

    gate, query_t, key_t, value_t, within, mid_gram, mid_memory, carried = call(
        functools.partial(prepare_kernel, total=total, width=width),
        head_count // step,
        [smem, smem, step_block(rows), step_block(shard), step_block(shard), full(head_count, shard)],
        [
            head_block(rows, rows),
            head_block(width, rows),
            head_block(width, rows),
            head_block(width, rows),
            head_block(width, rows),
            head_block(half + PAD, width),
            head_block(width, width),
            full(head_count, rows),
        ],
        [
            per_head(rows, rows),
            per_head(width, rows, dtype=bf16),
            per_head(width, rows, dtype=bf16),
            per_head(width, rows, dtype=bf16),
            per_head(width, rows),
            per_head(half + PAD, width),
            per_head(width, width),
            per_head(rows),
        ],
        [
            pltpu.VMEM((head_count, shard), f32),
            pltpu.VMEM((shard, head_count), f32),
            pltpu.VMEM((head_count, shard), f32),
            pltpu.VMEM((head_count, width), f32),
        ],
        "prepare",
        4 << 30,
    )(where, doc_lengths, decay_rates, queries, key_vectors, value_vectors, bins)

    own_decay = gram_sum[:, half + 1 : half + 2, :]
    body = (jnp.arange(half + PAD) < half + 1)[None, :, None]
    gram_prior = memory_prior = None
    covered = 0
    while covered < seq - 1:
        if covered == 0:
            hop = functools.partial(lax.ppermute, axis_name="seq", perm=[(i, i + 1) for i in range(seq - 1)])
            gram_prior, memory_prior = hop(gram_sum), hop(memory_sum)
            covered = 1
        else:
            shift = covered + 1
            hop = functools.partial(
                lax.ppermute, axis_name="seq", perm=[(i, i + shift) for i in range(seq - shift)]
            )
            prior_decay = gram_prior[:, half + 1 : half + 2, :]
            gram_in = hop(jnp.where(body, gram_sum, 0.0) + own_decay * gram_prior)
            memory_in = hop(memory_sum + own_decay * memory_prior)
            gram_prior = jnp.where(body, gram_prior, 0.0) + prior_decay * gram_in
            covered = covered + shift
            if covered < seq - 1:
                memory_prior = memory_prior + prior_decay * memory_in

    def swap(x):
        return lax.ppermute(x, "sub", [(i, (i + 1) % cores) for i in range(cores)])

    steps = heads // step
    solved = []
    for turn in range(cores):

        def group_index(i, where_ref, turn=turn):
            return lax.rem(where_ref[1] + turn, cores) * steps + i

        def block(*shape):
            return pl.BlockSpec(
                (step, *shape), lambda i, where_ref: (group_index(i, where_ref),) + (0,) * len(shape)
            )

        def local_block(*shape):
            return pl.BlockSpec((step, *shape), lambda i, where_ref: (i,) + (0,) * len(shape))

        solved.append(
            call(
                functools.partial(solve_kernel, cores=cores, turn=turn, width=width),
                steps,
                [
                    smem,
                    pl.BlockSpec((shard, step * width), lambda i, where_ref: (0, group_index(i, where_ref))),
                    block(rows, rows),
                    block(width, rows),
                    block(width, rows),
                    block(width, rows),
                    block(width, rows),
                    block(half + PAD, width),
                    full(head_count, rows),
                    local_block(half + PAD, width),
                ],
                [local_block(rows, 2 * width), local_block(rows, width)],
                [
                    jax.ShapeDtypeStruct((heads, rows, 2 * width), bf16),
                    jax.ShapeDtypeStruct((heads, rows, width), f32),
                ],
                [],
                f"solve_{turn}",
                2 << 30,
            )(
                where, ridge_terms, key_vectors, gate, query_t, key_t, value_t, within, mid_gram, carried,
                gram_prior if turn == 0 else swap(gram_prior),
            )
        )

    if covered > 1:
        solved, memory_in = lax.optimization_barrier((solved, memory_in))
        memory_prior = memory_prior + prior_decay * memory_in
    output = None
    for turn in range(cores):

        def group_all(*shape, turn=turn):
            return pl.BlockSpec(
                (heads, *shape),
                lambda i, where_ref: (lax.rem(where_ref[1] + turn, cores),) + (0,) * len(shape),
            )

        in_specs = [
            full(heads, rows, 2 * width),
            full(heads, rows, width),
            pl.BlockSpec(
                (heads, PAD, width),
                lambda i, where_ref, turn=turn: (lax.rem(where_ref[1] + turn, cores), half // PAD, 0),
            ),
            group_all(width, width),
            full(heads, width, width),
        ]
        operands = [where, *solved[turn], mid_gram, mid_memory, memory_prior if turn == 0 else swap(memory_prior)]
        aliases = {}
        if output is not None:
            aliases = {len(operands): 0}
            in_specs.append(any_space)
            operands.append(output)
        output = call(
            functools.partial(read_kernel, width=width),
            1,
            in_specs,
            pl.BlockSpec(
                (rows, heads * width), lambda i, where_ref, turn=turn: (0, lax.rem(where_ref[1] + turn, cores))
            ),
            jax.ShapeDtypeStruct((rows, head_count * width), bf16),
            [],
            f"read_{turn}",
            1 << 28,
            input_output_aliases=aliases,
        )(*operands)
    return output


def solution(mesh):
    in_specs = (
        P(("rep", "seq", "sub"), "head"),
        P(("rep", "seq"), "head"),
        P(("rep", "seq"), "head"),
        P(("rep", "seq"), "head"),
        P("rep"),
        P("head"),
        P("head"),
    )
    out_specs = P(("rep", "seq", "sub"), "head")
    return jax.shard_map(per_device, mesh=mesh, in_specs=in_specs, out_specs=out_specs, check_vma=False)
```

```python
import functools

import jax
import jax.numpy as jnp
from jax import lax
from jax.experimental import pallas as pl
from jax.experimental.pallas import tpu as pltpu
from jax.sharding import PartitionSpec as P

ITERS = 4
guard = 1e-06
f32 = jnp.float32
bf16 = jnp.bfloat16
PAD = 8
PER_STEP = 4
VMEM = 24 << 20


def dot_nn(a, b):
    return lax.dot_general(a, b, (((1,), (0,)), ((), ())), preferred_element_type=f32)


def dot_nt(a, b):
    return lax.dot_general(a, b, (((1,), (1,)), ((), ())), preferred_element_type=f32)


def split(x):
    high = x.astype(bf16)
    low = (x - high.astype(f32)).astype(bf16)
    return high, low


def iota(shape, axis):
    return lax.broadcasted_iota(jnp.int32, shape, axis)


def doc_of(doc_ref, position):
    count = jnp.zeros_like(position)
    start = jnp.int32(0)
    for index in range(doc_ref.shape[0]):
        count = count + (start <= position).astype(jnp.int32)
        start = start + doc_ref[index]
    return count


def split_bins(bins):
    whole = bins.astype(f32)
    high = jnp.floor(whole * (1.0 / 128.0))
    low = whole - 128.0 * high
    return high.astype(bf16), low.astype(bf16)


def running_rows(bins):
    size = bins.shape[1]
    high, low = split_bins(bins)
    step = jnp.where(iota((size, size), 0) <= iota((size, size), 1), 1.0, 0.0).astype(bf16)
    return 128.0 * dot_nn(high, step) + dot_nn(low, step)


def running_columns(bins):
    size = bins.shape[1]
    high, low = split_bins(bins)
    step = jnp.where(iota((size, size), 1) <= iota((size, size), 0), 1.0, 0.0).astype(bf16)
    return 128.0 * dot_nt(step, high) + dot_nt(step, low)


def scale_column(rate_ref, total):
    count = rate_ref.shape[0]
    column = jnp.zeros((count, 1), f32)
    for head in range(count):
        column = jnp.where(iota((count, 1), 0) == head, rate_ref[head], column)
    return column * (-1.0 / total)


def weighted_sums(key_t, weight, both):
    width = key_t.shape[0]
    product = dot_nn(jnp.concatenate(split(key_t.astype(f32) * weight), 0), both)
    return product[:width] + product[width:]


def pack_gram(gram, decay):
    width = gram.shape[0]
    half = width // 2
    turned = pltpu.roll(gram[half:], half, 1)
    row, col = iota((half, width), 0), iota((half, width), 1)
    packed = jnp.where((col < half) & (row > col), turned, gram[:half])
    diagonal = jnp.sum(jnp.where(row == col, turned, 0.0), axis=0, keepdims=True)
    tail = jnp.where(iota((PAD, width), 0) == 0, diagonal, decay)
    return packed, tail


def unpack_gram(packed, diagonal):
    half, width = packed.shape
    turned = pltpu.roll(packed, half, 1)
    crossed = jnp.concatenate([packed, turned], 0).T
    row, col = iota((half, width), 0), iota((half, width), 1)
    top = jnp.where(row <= col, packed, crossed[:half])
    low_col = col - half
    bottom = jnp.where((low_col >= 0) & (row > low_col), turned, crossed[half:])
    bottom = jnp.where(row == low_col, pltpu.roll(jnp.broadcast_to(diagonal, (half, width)), half, 1), bottom)
    return jnp.concatenate([top, bottom], 0)


def sums_kernel(
    where_ref, doc_ref, rate_ref, key_hbm, value_hbm, bins_ref, gram_ref, memory_ref, *rest,
    total, heads, width, cut,
):
    weight_ref, decay_ref, both_ref, sems = rest[-4:]
    shard = key_hbm.shape[0]
    first = where_ref[0] * shard
    core = where_ref[1]
    copies = []
    for i in range(heads):
        cols = pl.ds(pl.multiple_of((core * heads + i) * width, width), width)
        for part, source in enumerate((key_hbm, value_hbm)):
            target = both_ref.at[part, i]
            copies.append(pltpu.make_async_copy(source.at[:, cols], target, sems.at[i, part]))
            copies[-1].start()
    scale = scale_column(rate_ref, total)
    cumulative = running_rows(bins_ref[...])
    last = cumulative[:, shard - 1 :]
    position = first + iota((1, shard), 1)
    end_doc = doc_of(doc_ref, first + shard - 1)
    weight_ref[...] = jnp.where(
        doc_of(doc_ref, position) == end_doc, jnp.exp(scale * (last - cumulative)), 0.0
    )
    through = end_doc == doc_of(doc_ref, first - 1)
    decay_ref[...] = jnp.broadcast_to(jnp.where(through, jnp.exp(scale * last), 0.0), decay_ref.shape)
    for i in range(heads):
        head = core * heads + i
        copies[2 * i].wait()
        copies[2 * i + 1].wait()
        key = both_ref[0, i]
        both = jnp.concatenate([key, both_ref[1, i]], 1)
        sums = weighted_sums(key.T, weight_ref[pl.ds(head, 1), :], both)
        state = jnp.concatenate(pack_gram(sums[:, :width], decay_ref[pl.ds(head, 1), :]), 0)
        if cut == 0:
            gram_ref[i] = state
            memory_ref[i] = sums[:, width:]
        else:
            gram_second, memory_second, gram_sent, memory_sent = rest[:4]
            at = i % cut
            (gram_ref if i < cut else gram_second)[at] = state
            (memory_ref if i < cut else memory_second)[at] = sums[:, width:]

            @pl.when((where_ref[0] == 1) == (i >= cut))
            def _(at=at, state=state, sums=sums):
                gram_sent[at] = state
                memory_sent[at] = sums[:, width:]


def between_kernel(
    where_ref, first_ref, second_ref, near_ref, far_ref, gram_first, gram_second, gram_near,
    ahead_ref, sent_ref, joined_ref, *, half,
):
    place = where_ref[0]
    line = slice(half + 1, half + 2)
    for i in range(first_ref.shape[0]):
        near = near_ref[i]
        ahead = first_ref[i] + gram_first[i, line, :] * near
        joined = near + gram_near[i, line, :] * far_ref[i]
        second = second_ref[i]
        behind = second + gram_second[i, line, :] * joined
        ahead_ref[i] = ahead
        joined_ref[i] = joined
        sent_ref[i] = jnp.where(place == 1, ahead, jnp.where(place == 2, behind, second))


def gather_kernel(where_ref, near_ref, joined_ref, nearer_ref, farther_ref, gram_near, prior_ref, *, half):
    place = where_ref[0]
    cut = near_ref.shape[0]
    line = slice(half + 1, half + 2)
    for i in range(cut):
        nearer = nearer_ref[i]
        own = near_ref[i] + gram_near[i, line, :] * farther_ref[i]
        prior_ref[i] = jnp.where(place == 2, nearer, own)
        prior_ref[cut + i] = jnp.where(place == 2, joined_ref[i], nearer)


def prepare_kernel(
    where_ref, doc_ref, rate_ref, query_ref, key_ref, value_ref, bins_ref,
    gate_ref, query_t_ref, key_t_ref, value_t_ref, within_ref, mid_gram_ref, mid_memory_ref, carried_ref,
    row_ref, column_ref, mid_ref, decay_ref, *, total, width,
):
    shard, rows = key_ref.shape[0], query_ref.shape[0]
    first = where_ref[0] * shard
    start = where_ref[1] * rows
    own = pl.ds(pl.multiple_of(start, rows), rows)
    before_doc = doc_of(doc_ref, first + start - 1)
    key_pos = first + start + iota((rows, 1), 0)
    own_pos = first + start + iota((1, rows), 1)
    own_doc = doc_of(doc_ref, own_pos)

    @pl.when(pl.program_id(0) == 0)
    def _():
        scale = scale_column(rate_ref, total)
        bins = bins_ref[...]
        cumulative = running_rows(bins)
        row_ref[...] = cumulative
        column_ref[...] = running_columns(bins)
        token = iota((1, shard), 1)
        before = jnp.sum(jnp.where(token == start - 1, cumulative, 0.0), axis=1, keepdims=True)
        mid_live = (token < start) & (doc_of(doc_ref, first + token) == before_doc)
        mid_ref[...] = jnp.where(
            mid_live, jnp.exp(scale * jnp.maximum(before - cumulative, 0.0)), 0.0
        )
        through = before_doc == doc_of(doc_ref, first - 1)
        decay_ref[...] = jnp.broadcast_to(
            jnp.where(through, jnp.exp(scale * before), 0.0), decay_ref.shape
        )
        carried_ref[...] = jnp.where(
            own_doc == before_doc, jnp.exp(scale * jnp.maximum(row_ref[:, own] - before, 0.0)), 0.0
        )

    allowed = (key_pos <= own_pos) & (doc_of(doc_ref, key_pos) == own_doc)
    columns = column_ref[own, :]
    for i in range(query_ref.shape[1] // width):
        head = pl.program_id(0) * PER_STEP + i
        scale = rate_ref[head] * (-1.0 / total)
        cols = slice(i * width, (i + 1) * width)
        key_t = key_ref[:, cols].T
        both = jnp.concatenate([key_ref[:, cols], value_ref[:, cols]], 1)
        sums = weighted_sums(key_t, mid_ref[pl.ds(head, 1), :], both)
        packed, tail = pack_gram(sums[:, :width], decay_ref[pl.ds(head, 1), :])
        mid_gram_ref[i, : width // 2, :] = packed
        mid_gram_ref[i, width // 2 :, :] = tail
        mid_memory_ref[i] = sums[:, width:]
        key_own = key_ref[own, cols]
        own_t = key_own.T
        query_t = query_ref[:, cols].T
        query_t_ref[i] = query_t
        key_t_ref[i] = own_t
        value_t_ref[i] = value_ref[own, cols].T
        column = jnp.sum(jnp.where(iota(columns.shape, 1) == head, columns, 0.0), axis=1, keepdims=True)
        gap = jnp.maximum(row_ref[pl.ds(head, 1), own] - column, 0.0)
        gate = jnp.where(allowed, jnp.exp(scale * gap), 0.0)
        gate_ref[i] = gate
        weighted = dot_nn(key_own, query_t) * gate
        within_ref[i] = dot_nn(jnp.concatenate([own_t, own_t], 1), jnp.concatenate(split(weighted), 0))


def solve_kernel(
    where_ref, ridge_ref, key_ref, gate_ref, query_t_ref, key_t_ref, value_t_ref, within_ref, mid_ref, carried_ref,
    gram_ref, solution_ref, chunk_ref, *, cores, turn, width,
):
    rows = query_t_ref.shape[2]
    core = where_ref[1]
    steps = pl.num_programs(0)
    group = lax.rem(core + turn, cores)
    own = pl.ds(pl.multiple_of(core * rows, rows), rows)
    half = width // 2
    step = gram_ref.shape[0] // steps
    skip = pl.program_id(0) * step
    per_step = range(step)
    base = group * gram_ref.shape[0] + skip

    def row_sum(x):
        return jnp.sum(x, axis=0, keepdims=True)

    def head_program(i):
        head = base + i
        cols = pl.ds(pl.multiple_of(head * width, width), width)
        ridge = ridge_ref[head]
        carried = carried_ref[pl.ds(head, 1), :]
        decay = mid_ref[head, half + 1 : half + 2, :]
        packed = mid_ref[head, :half, :] + decay * gram_ref[skip + i, :half, :]
        diagonal = mid_ref[head, half : half + 1, :] + decay * gram_ref[skip + i, half : half + 1, :]
        high, low = split(unpack_gram(packed, diagonal))
        system = jnp.concatenate(
            [jnp.concatenate([high, low], 0), jnp.concatenate([high, jnp.zeros_like(low)], 0)], 1
        )
        key = key_ref[own, cols]
        keys = jnp.concatenate([key, key], 1)
        key_pair = jnp.concatenate([key_t_ref[head], key_t_ref[head]], 1)
        query_t = query_t_ref[head]
        direction = query_t.astype(f32)
        residual = direction
        energy = row_sum(direction * direction)
        result = None
        yield
        for iteration in range(ITERS):
            last = iteration == ITERS - 1
            if iteration == 0:
                product = dot_nn(system[:, :width], query_t)
            else:
                pair = jnp.concatenate(split(direction), 0)
                plain = dot_nn(keys, pair)
                product = dot_nn(system, pair)
            yield
            if iteration > 0:
                weighted = plain * gate_ref[head]
                if not last:
                    weighted_pair = jnp.concatenate(split(weighted), 0)
            earlier = carried * (product[:width] + product[width:]) + ridge * direction
            yield
            if iteration == 0:
                applied = earlier + within_ref[head]
            elif not last:
                within = dot_nn(key_pair, weighted_pair)
                yield
                applied = earlier + within
            if last:
                curvature = row_sum(plain * weighted) + row_sum(direction * earlier)
            else:
                curvature = row_sum(direction * applied)
            stepsize = energy / (curvature + guard)
            moved = stepsize * direction
            result = moved if iteration == 0 else result + moved
            if not last:
                residual = residual - stepsize * applied
                energy_next = row_sum(residual * residual)
                direction = residual + (energy_next / (energy + guard)) * direction
                energy = energy_next
            yield
        plain = dot_nn(keys, jnp.concatenate(split(result), 0))
        high, low = split(carried * result)
        solution_ref[skip + i] = jnp.concatenate([high.T, low.T], 1)
        yield
        weighted_pair = jnp.concatenate(split(plain * gate_ref[head]), 0)
        yield
        value_t = value_t_ref[head]
        chunk = dot_nn(jnp.concatenate([value_t, value_t], 1), weighted_pair)
        yield
        chunk_ref[skip + i] = chunk.T

    programs = [head_program(i) for i in per_step]
    running = []
    while programs or running:
        if programs:
            running.append(programs.pop(0))
        for program in list(running):
            if next(program, running) is running:
                running.remove(program)


def read_kernel(where_ref, solution_ref, chunk_ref, mid_ref, mid_memory_ref, memory_ref, *rest, cores, turn, width):
    out_ref = rest[-1]
    half = width // 2
    heads = solution_ref.shape[0]
    base = lax.rem(where_ref[1] + turn, cores) * heads
    for i in range(heads):
        decay = mid_ref[base + i, half + 1 : half + 2, :]
        memory = mid_memory_ref[base + i] + decay * memory_ref[i]
        high, low = split(memory)
        pair = jnp.concatenate(
            [jnp.concatenate([high, high], 0), jnp.concatenate([low, jnp.zeros_like(low)], 0)], 1
        )
        product = dot_nn(solution_ref[i], pair)
        out = product[:, :width] + product[:, width:] + chunk_ref[i]
        out_ref[:, i * width : (i + 1) * width] = out.astype(out_ref.dtype)


def per_device(queries, key_vectors, value_vectors, gate_bins, doc_lengths, decay_rates, ridge_terms):
    head_count = decay_rates.shape[0]
    shard = key_vectors.shape[0]
    rows = queries.shape[0]
    width = key_vectors.shape[1] // head_count
    half = width // 2
    seq = lax.axis_size("seq")
    cores = lax.axis_size("sub")
    heads = head_count // cores
    total = shard * seq
    where = jnp.stack([lax.axis_index("seq"), lax.axis_index("sub")]).astype(jnp.int32)
    bins = gate_bins.T
    smem = pl.BlockSpec(memory_space=pltpu.SMEM)
    any_space = pl.BlockSpec(memory_space=pl.ANY)
    hbm = pl.BlockSpec(memory_space=pltpu.HBM)
    vmem = pl.BlockSpec(memory_space=pltpu.VMEM)

    def pinned(x):
        return pltpu.with_memory_space_constraint(x, pltpu.HBM)

    def full(*shape):
        return pl.BlockSpec(shape, lambda i, where_ref: (0,) * len(shape))

    def call(kernel, grid, in_specs, out_specs, out_shape, scratch, name, cost, **options):
        return pl.pallas_call(
            kernel,
            grid_spec=pltpu.PrefetchScalarGridSpec(
                num_scalar_prefetch=1,
                grid=(grid,),
                in_specs=in_specs,
                out_specs=out_specs,
                scratch_shapes=scratch,
            ),
            out_shape=out_shape,
            name=name,
            cost_estimate=pl.CostEstimate(flops=cost, bytes_accessed=4 << 20, transcendentals=0),
            compiler_params=pltpu.CompilerParams(vmem_limit_bytes=VMEM),
            **options,
        )

    cut = heads // 2 if seq == 4 and heads % 2 == 0 else 0
    part = cut or heads
    gram_shape = jax.ShapeDtypeStruct((part, half + PAD, width), f32)
    memory_shape = jax.ShapeDtypeStruct((part, width, width), f32)
    sums = call(
        functools.partial(sums_kernel, total=total, heads=heads, width=width, cut=cut),
        1,
        [smem, smem, hbm, hbm, full(head_count, shard)],
        [vmem] * (6 if cut else 2),
        [gram_shape, memory_shape] * (3 if cut else 1),
        [
            pltpu.VMEM((head_count, shard), f32),
            pltpu.VMEM((head_count, width), f32),
            pltpu.VMEM((2, heads, shard, width), bf16),
            pltpu.SemaphoreType.DMA((heads, 2)),
        ],
        "shard_sums",
        1 << 30,
    )(where, pinned(doc_lengths), pinned(decay_rates), pinned(key_vectors), pinned(value_vectors), pinned(bins))

    step = min(PER_STEP, heads)

    def head_block(*shape):
        return pl.BlockSpec((step, *shape), lambda i, where_ref: (i,) + (0,) * len(shape))

    def step_block(count):
        return pl.BlockSpec((count, step * width), lambda i, where_ref: (0, i))

    def per_head(*shape, dtype=f32):
        return jax.ShapeDtypeStruct((head_count, *shape), dtype)

    gate, query_t, key_t, value_t, within, mid_gram, mid_memory, carried = call(
        functools.partial(prepare_kernel, total=total, width=width),
        head_count // step,
        [smem, smem, step_block(rows), step_block(shard), step_block(shard), full(head_count, shard)],
        [
            head_block(rows, rows),
            head_block(width, rows),
            head_block(width, rows),
            head_block(width, rows),
            head_block(width, rows),
            head_block(half + PAD, width),
            head_block(width, width),
            full(head_count, rows),
        ],
        [
            per_head(rows, rows),
            per_head(width, rows, dtype=bf16),
            per_head(width, rows, dtype=bf16),
            per_head(width, rows, dtype=bf16),
            per_head(width, rows),
            per_head(half + PAD, width),
            per_head(width, width),
            per_head(rows),
        ],
        [
            pltpu.VMEM((head_count, shard), f32),
            pltpu.VMEM((shard, head_count), f32),
            pltpu.VMEM((head_count, shard), f32),
            pltpu.VMEM((head_count, width), f32),
        ],
        "prepare",
        4 << 30,
    )(where, doc_lengths, decay_rates, queries, key_vectors, value_vectors, bins)

    def hop(x, pairs):
        return lax.ppermute(x, "seq", pairs)

    def after(x, *others):
        return lax.optimization_barrier((x, others))[0]

    if cut:
        gram_first, memory_first, gram_second, memory_second, gram_sent, memory_sent = sums
        chain, jump, leap = [(0, 1), (1, 2), (2, 3)], [(0, 2)], [(1, 3)]

        def between(first, second, near, far):
            return call(
                functools.partial(between_kernel, half=half),
                1,
                [vmem] * 7,
                [vmem] * 3,
                [jax.ShapeDtypeStruct(first.shape, f32)] * 3,
                [],
                "between",
                1 << 20,
            )(where, first, second, near, far, gram_first, gram_second, gram_near)

        def gathered(near, joined, nearer, farther):
            return call(
                functools.partial(gather_kernel, half=half),
                1,
                [vmem] * 5,
                vmem,
                jax.ShapeDtypeStruct((heads, *near.shape[1:]), f32),
                [],
                "gather",
                1 << 20,
            )(where, near, joined, nearer, farther, gram_near)

        gram_near, gram_far = hop(gram_sent, chain), hop(gram_second, jump)
        memory_near, memory_far = hop(memory_sent, chain), hop(memory_second, jump)
        gram_ahead, gram_sent, gram_joined = between(gram_first, gram_second, gram_near, gram_far)
        gram_nearer, gram_farther = hop(gram_sent, chain), hop(gram_ahead, leap)
        gram_prior = gathered(gram_near, gram_joined, gram_nearer, gram_farther)
        memory_ahead, memory_sent, memory_joined = between(memory_first, memory_second, memory_near, memory_far)
        memory_sent, memory_ahead = after((memory_sent, memory_ahead), gram_nearer, gram_farther)
        memory_nearer, memory_farther = hop(memory_sent, chain), hop(memory_ahead, leap)

        def memory_at(*ready):
            nearer, farther = after((memory_nearer, memory_farther), *ready)
            return gathered(memory_near, memory_joined, nearer, farther)

    else:
        gram_sum, memory_sum = sums
        own_decay = gram_sum[:, half + 1 : half + 2, :]
        body = (jnp.arange(half + PAD) < half + 1)[None, :, None]
        gram_prior, memory_prior = jnp.zeros_like(gram_sum), jnp.zeros_like(memory_sum)
        covered = 0
        while covered < seq - 1:
            shift = covered + 1
            pairs = [(i, i + shift) for i in range(seq - shift)]
            if covered == 0:
                gram_prior, memory_prior = hop(gram_sum, pairs), hop(memory_sum, pairs)
            else:
                prior_decay = gram_prior[:, half + 1 : half + 2, :]
                gram_in = hop(jnp.where(body, gram_sum, 0.0) + own_decay * gram_prior, pairs)
                memory_in = hop(memory_sum + own_decay * memory_prior, pairs)
                gram_prior = jnp.where(body, gram_prior, 0.0) + prior_decay * gram_in
                memory_prior = memory_prior + prior_decay * memory_in
            covered = covered + shift

        def memory_at(*ready):
            return after(memory_prior, *ready)

    def swap(x):
        return lax.ppermute(x, "sub", [(i, (i + 1) % cores) for i in range(cores)])

    steps = heads // step
    solved = []
    for turn in range(cores):
        solved.append(
            call(
                functools.partial(solve_kernel, cores=cores, turn=turn, width=width),
                steps,
                [smem] + [vmem] * 9,
                [vmem] * 2,
                [
                    jax.ShapeDtypeStruct((heads, rows, 2 * width), bf16),
                    jax.ShapeDtypeStruct((heads, rows, width), f32),
                ],
                [],
                f"solve_{turn}",
                2 << 30,
            )(
                where, ridge_terms, key_vectors, gate, query_t, key_t, value_t, within, mid_gram, carried,
                gram_prior if turn == 0 else swap(gram_prior),
            )
        )

    memory_prior = memory_at(*solved)
    output = None
    for turn in range(cores):
        in_specs = [vmem] * 5
        operands = [where, *solved[turn], mid_gram, mid_memory, memory_prior if turn == 0 else swap(memory_prior)]
        aliases = {}
        if output is not None:
            aliases = {len(operands): 0}
            in_specs.append(any_space)
            operands.append(output)
        output = call(
            functools.partial(read_kernel, cores=cores, turn=turn, width=width),
            1,
            in_specs,
            pl.BlockSpec(
                (rows, heads * width), lambda i, where_ref, turn=turn: (0, lax.rem(where_ref[1] + turn, cores))
            ),
            jax.ShapeDtypeStruct((rows, head_count * width), bf16),
            [],
            f"read_{turn}",
            1 << 28,
            input_output_aliases=aliases,
        )(*operands)
    return output


def solution(mesh):
    in_specs = (
        P(("rep", "seq", "sub"), "head"),
        P(("rep", "seq"), "head"),
        P(("rep", "seq"), "head"),
        P(("rep", "seq"), "head"),
        P("rep"),
        P("head"),
        P("head"),
    )
    out_specs = P(("rep", "seq", "sub"), "head")
    return jax.shard_map(per_device, mesh=mesh, in_specs=in_specs, out_specs=out_specs, check_vma=False)
```

```python
import functools

import jax
import jax.numpy as jnp
from jax import lax
from jax.experimental import pallas as pl
from jax.experimental.pallas import tpu as pltpu
from jax.sharding import PartitionSpec as P

ITERS = 4
guard = 1e-06
f32 = jnp.float32
bf16 = jnp.bfloat16
PAD = 8
PER_STEP = 4
VMEM = 24 << 20


def dot_nn(a, b):
    return lax.dot_general(a, b, (((1,), (0,)), ((), ())), preferred_element_type=f32)


def dot_nt(a, b):
    return lax.dot_general(a, b, (((1,), (1,)), ((), ())), preferred_element_type=f32)


def split(x):
    high = x.astype(bf16)
    low = (x - high.astype(f32)).astype(bf16)
    return high, low


def iota(shape, axis):
    return lax.broadcasted_iota(jnp.int32, shape, axis)


def doc_of(doc_ref, position):
    count = jnp.zeros_like(position)
    start = jnp.int32(0)
    for index in range(doc_ref.shape[0]):
        count = count + (start <= position).astype(jnp.int32)
        start = start + doc_ref[index]
    return count


def split_bins(bins):
    whole = bins.astype(f32)
    high = jnp.floor(whole * (1.0 / 128.0))
    low = whole - 128.0 * high
    return high.astype(bf16), low.astype(bf16)


def running_rows(bins):
    size = bins.shape[1]
    high, low = split_bins(bins)
    step = jnp.where(iota((size, size), 0) <= iota((size, size), 1), 1.0, 0.0).astype(bf16)
    return 128.0 * dot_nn(high, step) + dot_nn(low, step)


def running_columns(bins):
    size = bins.shape[1]
    high, low = split_bins(bins)
    step = jnp.where(iota((size, size), 1) <= iota((size, size), 0), 1.0, 0.0).astype(bf16)
    return 128.0 * dot_nt(step, high) + dot_nt(step, low)


def scale_column(rate_ref, total):
    count = rate_ref.shape[0]
    column = jnp.zeros((count, 1), f32)
    for head in range(count):
        column = jnp.where(iota((count, 1), 0) == head, rate_ref[head], column)
    return column * (-1.0 / total)


def weighted_sums(key_t, weight, both):
    width = key_t.shape[0]
    product = dot_nn(jnp.concatenate(split(key_t.astype(f32) * weight), 0), both)
    return product[:width] + product[width:]


def pack_gram(gram, decay):
    width = gram.shape[0]
    half = width // 2
    turned = pltpu.roll(gram[half:], half, 1)
    row, col = iota((half, width), 0), iota((half, width), 1)
    packed = jnp.where((col < half) & (row > col), turned, gram[:half])
    diagonal = jnp.sum(jnp.where(row == col, turned, 0.0), axis=0, keepdims=True)
    tail = jnp.where(iota((PAD, width), 0) == 0, diagonal, decay)
    return packed, tail


def unpack_gram(packed, diagonal):
    half, width = packed.shape
    turned = pltpu.roll(packed, half, 1)
    crossed = jnp.concatenate([packed, turned], 0).T
    row, col = iota((half, width), 0), iota((half, width), 1)
    top = jnp.where(row <= col, packed, crossed[:half])
    low_col = col - half
    bottom = jnp.where((low_col >= 0) & (row > low_col), turned, crossed[half:])
    bottom = jnp.where(row == low_col, pltpu.roll(jnp.broadcast_to(diagonal, (half, width)), half, 1), bottom)
    return jnp.concatenate([top, bottom], 0)


def sums_kernel(
    where_ref, doc_ref, rate_ref, key_hbm, value_hbm, bins_ref, gram_ref, memory_ref,
    weight_ref, decay_ref, both_ref, sems, *, total, heads, width,
):
    shard = key_hbm.shape[0]
    first = where_ref[0] * shard
    core = where_ref[1]
    copies = []
    for i in range(heads):
        cols = pl.ds(pl.multiple_of((core * heads + i) * width, width), width)
        for part, source in enumerate((key_hbm, value_hbm)):
            target = both_ref.at[part, i]
            copies.append(pltpu.make_async_copy(source.at[:, cols], target, sems.at[i, part]))
            copies[-1].start()
    scale = scale_column(rate_ref, total)
    cumulative = running_rows(bins_ref[...])
    last = cumulative[:, shard - 1 :]
    position = first + iota((1, shard), 1)
    end_doc = doc_of(doc_ref, first + shard - 1)
    weight_ref[...] = jnp.where(
        doc_of(doc_ref, position) == end_doc, jnp.exp(scale * (last - cumulative)), 0.0
    )
    through = end_doc == doc_of(doc_ref, first - 1)
    decay_ref[...] = jnp.broadcast_to(jnp.where(through, jnp.exp(scale * last), 0.0), decay_ref.shape)
    for i in range(heads):
        head = core * heads + i
        copies[2 * i].wait()
        copies[2 * i + 1].wait()
        key = both_ref[0, i]
        both = jnp.concatenate([key, both_ref[1, i]], 1)
        sums = weighted_sums(key.T, weight_ref[pl.ds(head, 1), :], both)
        state = jnp.concatenate(pack_gram(sums[:, :width], decay_ref[pl.ds(head, 1), :]), 0)
        gram_ref[i] = state
        memory_ref[i] = sums[:, width:]


def decay_line(gram_ref, i, half):
    return gram_ref[i, half + 1 : half + 2, :]


def include_kernel(where_ref, own_ref, before_ref, own_gram, before_gram, out_ref, *, half, fresh):
    received = (where_ref[0] & 1) == 1
    for i in range(own_ref.shape[0]):
        decay = decay_line(own_gram, i, half)
        state = own_ref[i] + decay * before_ref[i]
        if own_ref.shape[1] != own_ref.shape[2]:
            over = decay_line(before_gram, i, half)
            over = jnp.where(received, over, 1.0) if fresh else over
            state = jnp.where(iota(state.shape, 0) > half, decay * over, state)
        out_ref[i] = state


def extend_kernel(where_ref, before_ref, before_gram, *rest, half, bit, fresh):
    out_ref = rest[-1]
    first_received = (where_ref[0] & 1) == 1
    received = ((where_ref[0] >> bit) & 1) == 1
    for i in range(before_ref.shape[0]):
        arrived = rest[0][i]
        for other in rest[1:-1]:
            arrived = arrived + other[i]
        over = decay_line(before_gram, i, half)
        over = jnp.where(first_received, over, 1.0) if fresh else over
        state = before_ref[i] + over * arrived
        if before_ref.shape[1] != before_ref.shape[2]:
            passed = jnp.where(received, over * arrived[half + 1 : half + 2], over)
            state = jnp.where(iota(state.shape, 0) > half, passed, state)
        out_ref[i] = state


def prepare_kernel(
    where_ref, doc_ref, rate_ref, query_ref, key_ref, value_ref, bins_ref,
    gate_ref, query_t_ref, key_t_ref, value_t_ref, within_ref, mid_gram_ref, mid_memory_ref, carried_ref,
    row_ref, column_ref, mid_ref, decay_ref, *, total, width,
):
    shard, rows = key_ref.shape[0], query_ref.shape[0]
    first = where_ref[0] * shard
    start = where_ref[1] * rows
    own = pl.ds(pl.multiple_of(start, rows), rows)
    before_doc = doc_of(doc_ref, first + start - 1)
    key_pos = first + start + iota((rows, 1), 0)
    own_pos = first + start + iota((1, rows), 1)
    own_doc = doc_of(doc_ref, own_pos)

    @pl.when(pl.program_id(0) == 0)
    def _():
        scale = scale_column(rate_ref, total)
        bins = bins_ref[...]
        cumulative = running_rows(bins)
        row_ref[...] = cumulative
        column_ref[...] = running_columns(bins)
        token = iota((1, shard), 1)
        before = jnp.sum(jnp.where(token == start - 1, cumulative, 0.0), axis=1, keepdims=True)
        mid_live = (token < start) & (doc_of(doc_ref, first + token) == before_doc)
        mid_ref[...] = jnp.where(
            mid_live, jnp.exp(scale * jnp.maximum(before - cumulative, 0.0)), 0.0
        )
        through = before_doc == doc_of(doc_ref, first - 1)
        decay_ref[...] = jnp.broadcast_to(
            jnp.where(through, jnp.exp(scale * before), 0.0), decay_ref.shape
        )
        carried_ref[...] = jnp.where(
            own_doc == before_doc, jnp.exp(scale * jnp.maximum(row_ref[:, own] - before, 0.0)), 0.0
        )

    allowed = (key_pos <= own_pos) & (doc_of(doc_ref, key_pos) == own_doc)
    columns = column_ref[own, :]
    for i in range(query_ref.shape[1] // width):
        head = pl.program_id(0) * PER_STEP + i
        scale = rate_ref[head] * (-1.0 / total)
        cols = slice(i * width, (i + 1) * width)
        key_t = key_ref[:, cols].T
        both = jnp.concatenate([key_ref[:, cols], value_ref[:, cols]], 1)
        sums = weighted_sums(key_t, mid_ref[pl.ds(head, 1), :], both)
        packed, tail = pack_gram(sums[:, :width], decay_ref[pl.ds(head, 1), :])
        mid_gram_ref[i, : width // 2, :] = packed
        mid_gram_ref[i, width // 2 :, :] = tail
        mid_memory_ref[i] = sums[:, width:]
        key_own = key_ref[own, cols]
        own_t = key_own.T
        query_t = query_ref[:, cols].T
        query_t_ref[i] = query_t
        key_t_ref[i] = own_t
        value_t_ref[i] = value_ref[own, cols].T
        column = jnp.sum(jnp.where(iota(columns.shape, 1) == head, columns, 0.0), axis=1, keepdims=True)
        gap = jnp.maximum(row_ref[pl.ds(head, 1), own] - column, 0.0)
        gate = jnp.where(allowed, jnp.exp(scale * gap), 0.0)
        gate_ref[i] = gate
        weighted = dot_nn(key_own, query_t) * gate
        within_ref[i] = dot_nn(jnp.concatenate([own_t, own_t], 1), jnp.concatenate(split(weighted), 0))


def solve_kernel(
    where_ref, ridge_ref, key_ref, gate_ref, query_t_ref, key_t_ref, value_t_ref, within_ref, mid_ref, carried_ref,
    gram_ref, solution_ref, chunk_ref, *, cores, turn, width,
):
    rows = query_t_ref.shape[2]
    core = where_ref[1]
    steps = pl.num_programs(0)
    group = lax.rem(core + turn, cores)
    own = pl.ds(pl.multiple_of(core * rows, rows), rows)
    half = width // 2
    step = gram_ref.shape[0] // steps
    skip = pl.program_id(0) * step
    per_step = range(step)
    base = group * gram_ref.shape[0] + skip

    def row_sum(x):
        return jnp.sum(x, axis=0, keepdims=True)

    def head_program(i):
        head = base + i
        cols = pl.ds(pl.multiple_of(head * width, width), width)
        ridge = ridge_ref[head]
        carried = carried_ref[pl.ds(head, 1), :]
        decay = mid_ref[head, half + 1 : half + 2, :]
        packed = mid_ref[head, :half, :] + decay * gram_ref[skip + i, :half, :]
        diagonal = mid_ref[head, half : half + 1, :] + decay * gram_ref[skip + i, half : half + 1, :]
        high, low = split(unpack_gram(packed, diagonal))
        system = jnp.concatenate(
            [jnp.concatenate([high, low], 0), jnp.concatenate([high, jnp.zeros_like(low)], 0)], 1
        )
        key = key_ref[own, cols]
        keys = jnp.concatenate([key, key], 1)
        key_pair = jnp.concatenate([key_t_ref[head], key_t_ref[head]], 1)
        query_t = query_t_ref[head]
        direction = query_t.astype(f32)
        residual = direction
        energy = row_sum(direction * direction)
        result = None
        yield
        for iteration in range(ITERS):
            last = iteration == ITERS - 1
            if iteration == 0:
                product = dot_nn(system[:, :width], query_t)
            else:
                pair = jnp.concatenate(split(direction), 0)
                plain = dot_nn(keys, pair)
                product = dot_nn(system, pair)
            yield
            if iteration > 0:
                weighted = plain * gate_ref[head]
                if not last:
                    weighted_pair = jnp.concatenate(split(weighted), 0)
            earlier = carried * (product[:width] + product[width:]) + ridge * direction
            yield
            if iteration == 0:
                applied = earlier + within_ref[head]
            elif not last:
                within = dot_nn(key_pair, weighted_pair)
                yield
                applied = earlier + within
            if last:
                curvature = row_sum(plain * weighted) + row_sum(direction * earlier)
            else:
                curvature = row_sum(direction * applied)
            stepsize = energy / (curvature + guard)
            moved = stepsize * direction
            result = moved if iteration == 0 else result + moved
            if not last:
                residual = residual - stepsize * applied
                energy_next = row_sum(residual * residual)
                direction = residual + (energy_next / (energy + guard)) * direction
                energy = energy_next
            yield
        plain = dot_nn(keys, jnp.concatenate(split(result), 0))
        high, low = split(carried * result)
        solution_ref[skip + i] = jnp.concatenate([high.T, low.T], 1)
        yield
        weighted_pair = jnp.concatenate(split(plain * gate_ref[head]), 0)
        yield
        value_t = value_t_ref[head]
        chunk = dot_nn(jnp.concatenate([value_t, value_t], 1), weighted_pair)
        yield
        chunk_ref[skip + i] = chunk.T

    programs = [head_program(i) for i in per_step]
    running = []
    while programs or running:
        if programs:
            running.append(programs.pop(0))
        for program in list(running):
            if next(program, running) is running:
                running.remove(program)


def read_kernel(where_ref, solution_ref, chunk_ref, mid_ref, mid_memory_ref, memory_ref, *rest, cores, turn, width):
    out_ref = rest[-1]
    half = width // 2
    heads = solution_ref.shape[0]
    base = lax.rem(where_ref[1] + turn, cores) * heads
    for i in range(heads):
        decay = mid_ref[base + i, half + 1 : half + 2, :]
        memory = mid_memory_ref[base + i] + decay * memory_ref[i]
        high, low = split(memory)
        pair = jnp.concatenate(
            [jnp.concatenate([high, high], 0), jnp.concatenate([low, jnp.zeros_like(low)], 0)], 1
        )
        product = dot_nn(solution_ref[i], pair)
        out = product[:, :width] + product[:, width:] + chunk_ref[i]
        out_ref[:, i * width : (i + 1) * width] = out.astype(out_ref.dtype)


def per_device(queries, key_vectors, value_vectors, gate_bins, doc_lengths, decay_rates, ridge_terms):
    head_count = decay_rates.shape[0]
    shard = key_vectors.shape[0]
    rows = queries.shape[0]
    width = key_vectors.shape[1] // head_count
    half = width // 2
    seq = lax.axis_size("seq")
    cores = lax.axis_size("sub")
    heads = head_count // cores
    total = shard * seq
    where = jnp.stack([lax.axis_index("seq"), lax.axis_index("sub")]).astype(jnp.int32)
    bins = gate_bins.T
    smem = pl.BlockSpec(memory_space=pltpu.SMEM)
    any_space = pl.BlockSpec(memory_space=pl.ANY)
    hbm = pl.BlockSpec(memory_space=pltpu.HBM)
    vmem = pl.BlockSpec(memory_space=pltpu.VMEM)

    def pinned(x):
        return pltpu.with_memory_space_constraint(x, pltpu.HBM)

    def full(*shape):
        return pl.BlockSpec(shape, lambda i, where_ref: (0,) * len(shape))

    def call(kernel, grid, in_specs, out_specs, out_shape, scratch, name, cost, **options):
        return pl.pallas_call(
            kernel,
            grid_spec=pltpu.PrefetchScalarGridSpec(
                num_scalar_prefetch=1,
                grid=(grid,),
                in_specs=in_specs,
                out_specs=out_specs,
                scratch_shapes=scratch,
            ),
            out_shape=out_shape,
            name=name,
            cost_estimate=pl.CostEstimate(flops=cost, bytes_accessed=4 << 20, transcendentals=0),
            compiler_params=pltpu.CompilerParams(vmem_limit_bytes=VMEM),
            **options,
        )

    gram_sum, memory_sum = call(
        functools.partial(sums_kernel, total=total, heads=heads, width=width),
        1,
        [smem, smem, hbm, hbm, full(head_count, shard)],
        [vmem] * 2,
        [
            jax.ShapeDtypeStruct((heads, half + PAD, width), f32),
            jax.ShapeDtypeStruct((heads, width, width), f32),
        ],
        [
            pltpu.VMEM((head_count, shard), f32),
            pltpu.VMEM((head_count, width), f32),
            pltpu.VMEM((2, heads, shard, width), bf16),
            pltpu.SemaphoreType.DMA((heads, 2)),
        ],
        "shard_sums",
        1 << 30,
    )(where, pinned(doc_lengths), pinned(decay_rates), pinned(key_vectors), pinned(value_vectors), pinned(bins))

    step = min(PER_STEP, heads)

    def head_block(*shape):
        return pl.BlockSpec((step, *shape), lambda i, where_ref: (i,) + (0,) * len(shape))

    def step_block(count):
        return pl.BlockSpec((count, step * width), lambda i, where_ref: (0, i))

    def per_head(*shape, dtype=f32):
        return jax.ShapeDtypeStruct((head_count, *shape), dtype)

    gate, query_t, key_t, value_t, within, mid_gram, mid_memory, carried = call(
        functools.partial(prepare_kernel, total=total, width=width),
        head_count // step,
        [smem, smem, step_block(rows), step_block(shard), step_block(shard), full(head_count, shard)],
        [
            head_block(rows, rows),
            head_block(width, rows),
            head_block(width, rows),
            head_block(width, rows),
            head_block(width, rows),
            head_block(half + PAD, width),
            head_block(width, width),
            full(head_count, rows),
        ],
        [
            per_head(rows, rows),
            per_head(width, rows, dtype=bf16),
            per_head(width, rows, dtype=bf16),
            per_head(width, rows, dtype=bf16),
            per_head(width, rows),
            per_head(half + PAD, width),
            per_head(width, width),
            per_head(rows),
        ],
        [
            pltpu.VMEM((head_count, shard), f32),
            pltpu.VMEM((shard, head_count), f32),
            pltpu.VMEM((head_count, shard), f32),
            pltpu.VMEM((head_count, width), f32),
        ],
        "prepare",
        4 << 30,
    )(where, doc_lengths, decay_rates, queries, key_vectors, value_vectors, bins)

    def after(x, *others):
        return lax.optimization_barrier((x, others))[0]

    def hops(x, size):
        got = []
        for offset in range(size):
            pairs = [
                (left + size - 1, left + size + offset)
                for left in range(0, seq, 2 * size)
                if left + size + offset < seq
            ]
            if pairs:
                got.append(lax.ppermute(x, "seq", pairs))
        return got

    def small(kernel, name, operands):
        return call(
            kernel,
            1,
            [vmem] * len(operands),
            vmem,
            jax.ShapeDtypeStruct(operands[0].shape, f32),
            [],
            name,
            1 << 20,
        )(where, *operands)

    def include(own, before, before_gram, fresh):
        kernel = functools.partial(include_kernel, half=half, fresh=fresh)
        return small(kernel, "include", [own, before, gram_sum, before_gram])

    def extend(before, before_gram, got, bit, fresh):
        kernel = functools.partial(extend_kernel, half=half, bit=bit, fresh=fresh)
        return small(kernel, "extend", [before, before_gram, *got])

    (gram_prior,), (memory_prior,) = hops(gram_sum, 1), hops(memory_sum, 1)
    size, bit = 2, 1
    pending = None
    while size < seq:
        fresh = bit == 1
        if pending is not None:
            memory_prior = extend(*pending)
        gram_got = hops(include(gram_sum, gram_prior, gram_prior, fresh), size)
        memory_got = hops(include(memory_sum, memory_prior, gram_prior, fresh), size)
        pending = (memory_prior, gram_prior, memory_got, bit, fresh)
        gram_prior = extend(gram_prior, gram_prior, gram_got, bit, fresh)
        size, bit = 2 * size, bit + 1

    def memory_at(*ready):
        if pending is None:
            return memory_prior
        before, before_gram, got, *rest = pending
        return extend(before, before_gram, after(got, *ready), *rest)

    def swap(x):
        return lax.ppermute(x, "sub", [(i, (i + 1) % cores) for i in range(cores)])

    steps = heads // step
    solved = []
    for turn in range(cores):
        solved.append(
            call(
                functools.partial(solve_kernel, cores=cores, turn=turn, width=width),
                steps,
                [smem] + [vmem] * 9,
                [vmem] * 2,
                [
                    jax.ShapeDtypeStruct((heads, rows, 2 * width), bf16),
                    jax.ShapeDtypeStruct((heads, rows, width), f32),
                ],
                [],
                f"solve_{turn}",
                2 << 30,
            )(
                where, ridge_terms, key_vectors, gate, query_t, key_t, value_t, within, mid_gram, carried,
                gram_prior if turn == 0 else swap(gram_prior),
            )
        )

    memory_prior = memory_at(*solved)
    output = None
    for turn in range(cores):
        in_specs = [vmem] * 5
        operands = [where, *solved[turn], mid_gram, mid_memory, memory_prior if turn == 0 else swap(memory_prior)]
        aliases = {}
        if output is not None:
            aliases = {len(operands): 0}
            in_specs.append(any_space)
            operands.append(output)
        output = call(
            functools.partial(read_kernel, cores=cores, turn=turn, width=width),
            1,
            in_specs,
            pl.BlockSpec(
                (rows, heads * width), lambda i, where_ref, turn=turn: (0, lax.rem(where_ref[1] + turn, cores))
            ),
            jax.ShapeDtypeStruct((rows, head_count * width), bf16),
            [],
            f"read_{turn}",
            1 << 28,
            input_output_aliases=aliases,
        )(*operands)
    return output


def solution(mesh):
    in_specs = (
        P(("rep", "seq", "sub"), "head"),
        P(("rep", "seq"), "head"),
        P(("rep", "seq"), "head"),
        P(("rep", "seq"), "head"),
        P("rep"),
        P("head"),
        P("head"),
    )
    out_specs = P(("rep", "seq", "sub"), "head")
    return jax.shard_map(per_device, mesh=mesh, in_specs=in_specs, out_specs=out_specs, check_vma=False)
```

```python
import functools

import jax
import jax.numpy as jnp
from jax import lax
from jax.experimental import pallas as pl
from jax.experimental.pallas import tpu as pltpu
from jax.sharding import PartitionSpec as P

ITERS = 4
guard = 1e-06
f32 = jnp.float32
bf16 = jnp.bfloat16
PAD = 8
PER_STEP = 4
BLOCK = 4
VMEM = 24 << 20


def dot_nn(a, b):
    return lax.dot_general(a, b, (((1,), (0,)), ((), ())), preferred_element_type=f32)


def dot_nt(a, b):
    return lax.dot_general(a, b, (((1,), (1,)), ((), ())), preferred_element_type=f32)


def split(x):
    high = x.astype(bf16)
    low = (x - high.astype(f32)).astype(bf16)
    return high, low


def iota(shape, axis):
    return lax.broadcasted_iota(jnp.int32, shape, axis)


def doc_of(doc_ref, position):
    count = jnp.zeros_like(position)
    start = jnp.int32(0)
    for index in range(doc_ref.shape[0]):
        count = count + (start <= position).astype(jnp.int32)
        start = start + doc_ref[index]
    return count


def split_bins(bins):
    whole = bins.astype(f32)
    high = jnp.floor(whole * (1.0 / 128.0))
    low = whole - 128.0 * high
    return high.astype(bf16), low.astype(bf16)


def running_rows(bins):
    size = bins.shape[1]
    high, low = split_bins(bins)
    step = jnp.where(iota((size, size), 0) <= iota((size, size), 1), 1.0, 0.0).astype(bf16)
    return 128.0 * dot_nn(high, step) + dot_nn(low, step)


def running_columns(bins):
    size = bins.shape[1]
    high, low = split_bins(bins)
    step = jnp.where(iota((size, size), 1) <= iota((size, size), 0), 1.0, 0.0).astype(bf16)
    return 128.0 * dot_nt(step, high) + dot_nt(step, low)


def scale_column(rate_ref, total):
    count = rate_ref.shape[0]
    column = jnp.zeros((count, 1), f32)
    for head in range(count):
        column = jnp.where(iota((count, 1), 0) == head, rate_ref[head], column)
    return column * (-1.0 / total)


def weighted_sums(key_t, weight, both):
    width = key_t.shape[0]
    product = dot_nn(jnp.concatenate(split(key_t.astype(f32) * weight), 0), both)
    return product[:width] + product[width:]


def pack_gram(gram):
    width = gram.shape[0]
    half = width // 2
    turned = pltpu.roll(gram[half:], half, 1)
    row, col = iota((half, width), 0), iota((half, width), 1)
    packed = jnp.where((col < half) & (row > col), turned, gram[:half])
    diagonal = jnp.sum(jnp.where(row == col, turned, 0.0), axis=0, keepdims=True)
    return packed, diagonal


def unpack_gram(packed, diagonal):
    half, width = packed.shape
    turned = pltpu.roll(packed, half, 1)
    crossed = jnp.concatenate([packed, turned], 0).T
    row, col = iota((half, width), 0), iota((half, width), 1)
    top = jnp.where(row <= col, packed, crossed[:half])
    low_col = col - half
    bottom = jnp.where((low_col >= 0) & (row > low_col), turned, crossed[half:])
    bottom = jnp.where(row == low_col, pltpu.roll(jnp.broadcast_to(diagonal, (half, width)), half, 1), bottom)
    return jnp.concatenate([top, bottom], 0)


def sums_kernel(
    where_ref, doc_ref, rate_ref, key_hbm, value_hbm, bins_ref, gram_ref, memory_ref,
    weight_ref, decay_ref, both_ref, sems, *, total, heads, width,
):
    shard = key_hbm.shape[0]
    half = width // 2
    first = where_ref[0] * shard
    core = where_ref[1]
    copies = []
    for i in range(heads):
        cols = pl.ds(pl.multiple_of((core * heads + i) * width, width), width)
        for part, source in enumerate((key_hbm, value_hbm)):
            target = both_ref.at[part, i]
            copies.append(pltpu.make_async_copy(source.at[:, cols], target, sems.at[i, part]))
            copies[-1].start()
    scale = scale_column(rate_ref, total)
    cumulative = running_rows(bins_ref[...])
    last = cumulative[:, shard - 1 :]
    position = first + iota((1, shard), 1)
    end_doc = doc_of(doc_ref, first + shard - 1)
    weight_ref[...] = jnp.where(
        doc_of(doc_ref, position) == end_doc, jnp.exp(scale * (last - cumulative)), 0.0
    )
    through = end_doc == doc_of(doc_ref, first - 1)
    decay_ref[...] = jnp.broadcast_to(jnp.where(through, jnp.exp(scale * last), 0.0), decay_ref.shape)
    for i in range(heads):
        head = core * heads + i
        copies[2 * i].wait()
        copies[2 * i + 1].wait()
        key = both_ref[0, i]
        both = jnp.concatenate([key, both_ref[1, i]], 1)
        sums = weighted_sums(key.T, weight_ref[pl.ds(head, 1), :], both)
        packed, diagonal = pack_gram(sums[:, :width])
        gram_ref[i * half : (i + 1) * half, :] = packed
        gram_ref[heads * half + i : heads * half + i + 1, :] = diagonal
        tail = heads * half + heads + i
        gram_ref[tail : tail + 1, :] = decay_ref[pl.ds(head, 1), :]
        memory_ref[i] = sums[:, width:]


def decay_line(gram_ref, i, heads):
    row = gram_ref.shape[0] - tail_rows(heads) + heads + i
    return gram_ref[row : row + 1, :]


def tail_rows(heads):
    return -(-2 * heads // 8) * 8


def gram_rows(i, heads, half):
    return (slice(i * half, (i + 1) * half), slice(heads * half + i, heads * half + i + 1))


def direct_kernel(where_ref, *rest, heads, half, block):
    got, out_ref = rest[:-1], rest[-1]
    out_ref[...] = jnp.zeros_like(out_ref)
    arrived = lax.rem(where_ref[0], block)
    for i in range(heads):
        decays = [decay_line(ref, i, heads) for ref in got]
        for rows in gram_rows(i, heads, half):
            state = got[-1][rows, :]
            for ref, decay in zip(got[-2::-1], decays[-2::-1]):
                state = ref[rows, :] + decay * state
            out_ref[rows, :] = state
        over = jnp.ones_like(decays[0])
        for place, decay in enumerate(decays):
            over = jnp.where(arrived > place, over * decay, over)
        line = heads * half + heads + i
        out_ref[line : line + 1, :] = over


def include_kernel(where_ref, own_ref, before_ref, own_gram, *rest, heads, half):
    out_ref = rest[-1]
    memory = len(own_ref.shape) == 3
    for i in range(heads):
        decay = decay_line(own_gram, i, heads)
        if memory:
            out_ref[i] = own_ref[i] + decay * before_ref[i]
            continue
        for rows in gram_rows(i, heads, half):
            out_ref[rows, :] = own_ref[rows, :] + decay * before_ref[rows, :]
        line = heads * half + heads + i
        out_ref[line : line + 1, :] = decay * decay_line(before_ref, i, heads)


def extend_kernel(where_ref, before_ref, before_gram, *rest, heads, half, bit, fresh):
    out_ref, got = rest[-1], rest[:-1]
    memory = len(before_ref.shape) == 3
    received = ((where_ref[0] >> bit) & 1) == 1
    for i in range(heads):
        over = decay_line(before_gram, i, heads)
        if fresh:
            over = jnp.where((where_ref[0] & 1) == 1, over, 1.0)
        if memory:
            out_ref[i] = before_ref[i] + over * functools.reduce(jnp.add, [ref[i] for ref in got])
            continue
        for rows in gram_rows(i, heads, half):
            arrived = functools.reduce(jnp.add, [ref[rows, :] for ref in got])
            out_ref[rows, :] = before_ref[rows, :] + over * arrived
        passed = functools.reduce(jnp.add, [decay_line(ref, i, heads) for ref in got])
        line = heads * half + heads + i
        out_ref[line : line + 1, :] = jnp.where(received, over * passed, over)


def prepare_kernel(
    where_ref, doc_ref, rate_ref, query_ref, key_ref, value_ref, bins_ref,
    gate_ref, query_t_ref, key_t_ref, value_t_ref, within_ref, mid_gram_ref, mid_memory_ref, carried_ref,
    row_ref, column_ref, mid_ref, decay_ref, *, total, width,
):
    shard, rows = key_ref.shape[0], query_ref.shape[0]
    first = where_ref[0] * shard
    start = where_ref[1] * rows
    own = pl.ds(pl.multiple_of(start, rows), rows)
    before_doc = doc_of(doc_ref, first + start - 1)
    key_pos = first + start + iota((rows, 1), 0)
    own_pos = first + start + iota((1, rows), 1)
    own_doc = doc_of(doc_ref, own_pos)

    @pl.when(pl.program_id(0) == 0)
    def _():
        scale = scale_column(rate_ref, total)
        bins = bins_ref[...]
        cumulative = running_rows(bins)
        row_ref[...] = cumulative
        column_ref[...] = running_columns(bins)
        token = iota((1, shard), 1)
        before = jnp.sum(jnp.where(token == start - 1, cumulative, 0.0), axis=1, keepdims=True)
        mid_live = (token < start) & (doc_of(doc_ref, first + token) == before_doc)
        mid_ref[...] = jnp.where(
            mid_live, jnp.exp(scale * jnp.maximum(before - cumulative, 0.0)), 0.0
        )
        through = before_doc == doc_of(doc_ref, first - 1)
        decay_ref[...] = jnp.broadcast_to(
            jnp.where(through, jnp.exp(scale * before), 0.0), decay_ref.shape
        )
        carried_ref[...] = jnp.where(
            own_doc == before_doc, jnp.exp(scale * jnp.maximum(row_ref[:, own] - before, 0.0)), 0.0
        )

    allowed = (key_pos <= own_pos) & (doc_of(doc_ref, key_pos) == own_doc)
    columns = column_ref[own, :]
    for i in range(query_ref.shape[1] // width):
        head = pl.program_id(0) * PER_STEP + i
        scale = rate_ref[head] * (-1.0 / total)
        cols = slice(i * width, (i + 1) * width)
        key_t = key_ref[:, cols].T
        both = jnp.concatenate([key_ref[:, cols], value_ref[:, cols]], 1)
        sums = weighted_sums(key_t, mid_ref[pl.ds(head, 1), :], both)
        packed, diagonal = pack_gram(sums[:, :width])
        mid_gram_ref[i, : width // 2, :] = packed
        mid_gram_ref[i, width // 2 :, :] = jnp.where(
            iota((PAD, width), 0) == 0, diagonal, decay_ref[pl.ds(head, 1), :]
        )
        mid_memory_ref[i] = sums[:, width:]
        key_own = key_ref[own, cols]
        own_t = key_own.T
        query_t = query_ref[:, cols].T
        query_t_ref[i] = query_t
        key_t_ref[i] = own_t
        value_t_ref[i] = value_ref[own, cols].T
        column = jnp.sum(jnp.where(iota(columns.shape, 1) == head, columns, 0.0), axis=1, keepdims=True)
        gap = jnp.maximum(row_ref[pl.ds(head, 1), own] - column, 0.0)
        gate = jnp.where(allowed, jnp.exp(scale * gap), 0.0)
        gate_ref[i] = gate
        weighted = dot_nn(key_own, query_t) * gate
        within_ref[i] = dot_nn(jnp.concatenate([own_t, own_t], 1), jnp.concatenate(split(weighted), 0))


def solve_kernel(
    where_ref, ridge_ref, key_ref, gate_ref, query_t_ref, key_t_ref, value_t_ref, within_ref, mid_ref, carried_ref,
    gram_ref, solution_ref, chunk_ref, *, cores, turn, width,
):
    rows = query_t_ref.shape[2]
    core = where_ref[1]
    heads = solution_ref.shape[0]
    group = lax.rem(core + turn, cores)
    own = pl.ds(pl.multiple_of(core * rows, rows), rows)
    half = width // 2
    base = group * heads

    def row_sum(x):
        return jnp.sum(x, axis=0, keepdims=True)

    def head_program(i):
        head = base + i
        cols = pl.ds(pl.multiple_of(head * width, width), width)
        ridge = ridge_ref[head]
        carried = carried_ref[pl.ds(head, 1), :]
        decay = mid_ref[head, half + 1 : half + 2, :]
        body, line = gram_rows(i, heads, half)
        packed = mid_ref[head, :half, :] + decay * gram_ref[body, :]
        diagonal = mid_ref[head, half : half + 1, :] + decay * gram_ref[line, :]
        high, low = split(unpack_gram(packed, diagonal))
        system = jnp.concatenate(
            [jnp.concatenate([high, low], 0), jnp.concatenate([high, jnp.zeros_like(low)], 0)], 1
        )
        key = key_ref[own, cols]
        keys = jnp.concatenate([key, key], 1)
        key_pair = jnp.concatenate([key_t_ref[head], key_t_ref[head]], 1)
        query_t = query_t_ref[head]
        direction = query_t.astype(f32)
        residual = direction
        energy = row_sum(direction * direction)
        result = None
        yield
        for iteration in range(ITERS):
            last = iteration == ITERS - 1
            if iteration == 0:
                product = dot_nn(system[:, :width], query_t)
            else:
                pair = jnp.concatenate(split(direction), 0)
                plain = dot_nn(keys, pair)
                product = dot_nn(system, pair)
            yield
            if iteration > 0:
                weighted = plain * gate_ref[head]
                if not last:
                    weighted_pair = jnp.concatenate(split(weighted), 0)
            earlier = carried * (product[:width] + product[width:]) + ridge * direction
            yield
            if iteration == 0:
                applied = earlier + within_ref[head]
            elif not last:
                within = dot_nn(key_pair, weighted_pair)
                yield
                applied = earlier + within
            if last:
                curvature = row_sum(plain * weighted) + row_sum(direction * earlier)
            else:
                curvature = row_sum(direction * applied)
            stepsize = energy / (curvature + guard)
            moved = stepsize * direction
            result = moved if iteration == 0 else result + moved
            if not last:
                residual = residual - stepsize * applied
                energy_next = row_sum(residual * residual)
                direction = residual + (energy_next / (energy + guard)) * direction
                energy = energy_next
            yield
        plain = dot_nn(keys, jnp.concatenate(split(result), 0))
        high, low = split(carried * result)
        solution_ref[i] = jnp.concatenate([high.T, low.T], 1)
        yield
        weighted_pair = jnp.concatenate(split(plain * gate_ref[head]), 0)
        yield
        value_t = value_t_ref[head]
        chunk = dot_nn(jnp.concatenate([value_t, value_t], 1), weighted_pair)
        yield
        chunk_ref[i] = chunk.T

    programs = [head_program(i) for i in range(heads)]
    running = []
    while programs or running:
        if programs:
            running.append(programs.pop(0))
        for program in list(running):
            if next(program, running) is running:
                running.remove(program)


def read_kernel(where_ref, solution_ref, chunk_ref, mid_ref, mid_memory_ref, memory_ref, *rest, cores, turn, width):
    out_ref = rest[-1]
    half = width // 2
    heads = solution_ref.shape[0]
    base = lax.rem(where_ref[1] + turn, cores) * heads
    for i in range(heads):
        decay = mid_ref[base + i, half + 1 : half + 2, :]
        memory = mid_memory_ref[base + i] + decay * memory_ref[i]
        high, low = split(memory)
        pair = jnp.concatenate(
            [jnp.concatenate([high, high], 0), jnp.concatenate([low, jnp.zeros_like(low)], 0)], 1
        )
        product = dot_nn(solution_ref[i], pair)
        out = product[:, :width] + product[:, width:] + chunk_ref[i]
        out_ref[:, i * width : (i + 1) * width] = out.astype(out_ref.dtype)


def per_device(queries, key_vectors, value_vectors, gate_bins, doc_lengths, decay_rates, ridge_terms):
    head_count = decay_rates.shape[0]
    shard = key_vectors.shape[0]
    rows = queries.shape[0]
    width = key_vectors.shape[1] // head_count
    half = width // 2
    seq = lax.axis_size("seq")
    cores = lax.axis_size("sub")
    heads = head_count // cores
    total = shard * seq
    where = jnp.stack([lax.axis_index("seq"), lax.axis_index("sub")]).astype(jnp.int32)
    bins = gate_bins.T
    smem = pl.BlockSpec(memory_space=pltpu.SMEM)
    any_space = pl.BlockSpec(memory_space=pl.ANY)
    hbm = pl.BlockSpec(memory_space=pltpu.HBM)
    vmem = pl.BlockSpec(memory_space=pltpu.VMEM)

    def pinned(x):
        return pltpu.with_memory_space_constraint(x, pltpu.HBM)

    def full(*shape):
        return pl.BlockSpec(shape, lambda i, where_ref: (0,) * len(shape))

    def call(kernel, grid, in_specs, out_specs, out_shape, scratch, name, cost, **options):
        return pl.pallas_call(
            kernel,
            grid_spec=pltpu.PrefetchScalarGridSpec(
                num_scalar_prefetch=1,
                grid=(grid,),
                in_specs=in_specs,
                out_specs=out_specs,
                scratch_shapes=scratch,
            ),
            out_shape=out_shape,
            name=name,
            cost_estimate=pl.CostEstimate(flops=cost, bytes_accessed=4 << 20, transcendentals=0),
            compiler_params=pltpu.CompilerParams(vmem_limit_bytes=VMEM),
            **options,
        )

    gram_sum, memory_sum = call(
        functools.partial(sums_kernel, total=total, heads=heads, width=width),
        1,
        [smem, smem, hbm, hbm, full(head_count, shard)],
        [vmem] * 2,
        [
            jax.ShapeDtypeStruct((heads * half + tail_rows(heads), width), f32),
            jax.ShapeDtypeStruct((heads, width, width), f32),
        ],
        [
            pltpu.VMEM((head_count, shard), f32),
            pltpu.VMEM((head_count, width), f32),
            pltpu.VMEM((2, heads, shard, width), bf16),
            pltpu.SemaphoreType.DMA((heads, 2)),
        ],
        "shard_sums",
        1 << 30,
    )(where, pinned(doc_lengths), pinned(decay_rates), pinned(key_vectors), pinned(value_vectors), pinned(bins))

    step = min(PER_STEP, heads)

    def head_block(*shape):
        return pl.BlockSpec((step, *shape), lambda i, where_ref: (i,) + (0,) * len(shape))

    def step_block(count):
        return pl.BlockSpec((count, step * width), lambda i, where_ref: (0, i))

    def per_head(*shape, dtype=f32):
        return jax.ShapeDtypeStruct((head_count, *shape), dtype)

    gate, query_t, key_t, value_t, within, mid_gram, mid_memory, carried = call(
        functools.partial(prepare_kernel, total=total, width=width),
        head_count // step,
        [smem, smem, step_block(rows), step_block(shard), step_block(shard), full(head_count, shard)],
        [
            head_block(rows, rows),
            head_block(width, rows),
            head_block(width, rows),
            head_block(width, rows),
            head_block(width, rows),
            head_block(half + PAD, width),
            head_block(width, width),
            full(head_count, rows),
        ],
        [
            per_head(rows, rows),
            per_head(width, rows, dtype=bf16),
            per_head(width, rows, dtype=bf16),
            per_head(width, rows, dtype=bf16),
            per_head(width, rows),
            per_head(half + PAD, width),
            per_head(width, width),
            per_head(rows),
        ],
        [
            pltpu.VMEM((head_count, shard), f32),
            pltpu.VMEM((shard, head_count), f32),
            pltpu.VMEM((head_count, shard), f32),
            pltpu.VMEM((head_count, width), f32),
        ],
        "prepare",
        4 << 30,
    )(where, doc_lengths, decay_rates, queries, key_vectors, value_vectors, bins)

    def after(x, *others):
        return lax.optimization_barrier((x, others))[0]

    def hops(x, size):
        got = []
        for offset in range(size):
            pairs = [
                (left + size - 1, left + size + offset)
                for left in range(0, seq, 2 * size)
                if left + size + offset < seq
            ]
            if pairs:
                got.append(lax.ppermute(x, "seq", pairs))
        return got

    def small(kernel, name, operands, **options):
        return call(
            functools.partial(kernel, heads=heads, half=half, **options),
            1,
            [vmem] * len(operands),
            vmem,
            jax.ShapeDtypeStruct(operands[0].shape, f32),
            [],
            name,
            1 << 20,
        )(where, *operands)

    block = min(BLOCK, seq)
    gram_near = [
        lax.ppermute(gram_sum, "seq", [(i, i + ahead) for i in range(seq - ahead) if i % block + ahead < block])
        for ahead in range(1, block)
    ]
    nearest = gram_near[0]
    (memory_prior,) = hops(memory_sum, 1)
    size, bit = 2, 1
    pending = gram_prior = None
    while size < seq:
        if pending is not None:
            memory_prior = small(extend_kernel, "extend", pending[0], **pending[1])
        if size >= block:
            if gram_prior is None:
                gram_prior = small(direct_kernel, "direct", gram_near, block=block)
            gram_got = hops(small(include_kernel, "include", [gram_sum, gram_prior, gram_sum]), size)
            before_gram = gram_prior
            gram_prior = small(
                extend_kernel, "extend", [gram_prior, gram_prior, *gram_got], bit=bit, fresh=False
            )
        else:
            before_gram = nearest
        included = small(include_kernel, "include", [memory_sum, memory_prior, gram_sum])
        memory_got = hops(included, size)
        if gram_prior is None:
            gram_near = after(gram_near, included)
        pending = [memory_prior, before_gram, *memory_got], {"bit": bit, "fresh": size < block}
        size, bit = 2 * size, bit + 1
    if gram_prior is None:
        gram_prior = small(direct_kernel, "direct", gram_near, block=block)

    def memory_at(*ready):
        if pending is None:
            return memory_prior
        (before, before_gram, *got), options = pending
        return small(extend_kernel, "extend", [before, before_gram, *after(got, *ready)], **options)

    def swap(x):
        return lax.ppermute(x, "sub", [(i, (i + 1) % cores) for i in range(cores)])

    solved = []
    for turn in range(cores):
        solved.append(
            call(
                functools.partial(solve_kernel, cores=cores, turn=turn, width=width),
                1,
                [smem] + [vmem] * 9,
                [vmem] * 2,
                [
                    jax.ShapeDtypeStruct((heads, rows, 2 * width), bf16),
                    jax.ShapeDtypeStruct((heads, rows, width), f32),
                ],
                [],
                f"solve_{turn}",
                2 << 30,
            )(
                where, ridge_terms, key_vectors, gate, query_t, key_t, value_t, within, mid_gram, carried,
                gram_prior if turn == 0 else swap(gram_prior),
            )
        )

    memory_prior = memory_at(*solved)
    output = None
    for turn in range(cores):
        in_specs = [vmem] * 5
        operands = [where, *solved[turn], mid_gram, mid_memory, memory_prior if turn == 0 else swap(memory_prior)]
        aliases = {}
        if output is not None:
            aliases = {len(operands): 0}
            in_specs.append(any_space)
            operands.append(output)
        output = call(
            functools.partial(read_kernel, cores=cores, turn=turn, width=width),
            1,
            in_specs,
            pl.BlockSpec(
                (rows, heads * width), lambda i, where_ref, turn=turn: (0, lax.rem(where_ref[1] + turn, cores))
            ),
            jax.ShapeDtypeStruct((rows, head_count * width), bf16),
            [],
            f"read_{turn}",
            1 << 28,
            input_output_aliases=aliases,
        )(*operands)
    return output


def solution(mesh):
    in_specs = (
        P(("rep", "seq", "sub"), "head"),
        P(("rep", "seq"), "head"),
        P(("rep", "seq"), "head"),
        P(("rep", "seq"), "head"),
        P("rep"),
        P("head"),
        P("head"),
    )
    out_specs = P(("rep", "seq", "sub"), "head")
    return jax.shard_map(per_device, mesh=mesh, in_specs=in_specs, out_specs=out_specs, check_vma=False)
```

```python
import functools

import jax
import jax.numpy as jnp
from jax import lax
from jax.experimental import pallas as pl
from jax.experimental.pallas import tpu as pltpu
from jax.sharding import PartitionSpec as P

ITERS = 4
guard = 1e-06
f32 = jnp.float32
bf16 = jnp.bfloat16
PAD = 8
PER_STEP = 4
VMEM = 24 << 20


def dot_nn(a, b):
    return lax.dot_general(a, b, (((1,), (0,)), ((), ())), preferred_element_type=f32)


def dot_nt(a, b):
    return lax.dot_general(a, b, (((1,), (1,)), ((), ())), preferred_element_type=f32)


def split(x):
    high = x.astype(bf16)
    low = (x - high.astype(f32)).astype(bf16)
    return high, low


def iota(shape, axis):
    return lax.broadcasted_iota(jnp.int32, shape, axis)


def doc_of(doc_ref, position):
    count = jnp.zeros_like(position)
    start = jnp.int32(0)
    for index in range(doc_ref.shape[0]):
        count = count + (start <= position).astype(jnp.int32)
        start = start + doc_ref[index]
    return count


def split_bins(bins):
    whole = bins.astype(f32)
    high = jnp.floor(whole * (1.0 / 128.0))
    low = whole - 128.0 * high
    return high.astype(bf16), low.astype(bf16)


def running_rows(bins):
    size = bins.shape[1]
    high, low = split_bins(bins)
    step = jnp.where(iota((size, size), 0) <= iota((size, size), 1), 1.0, 0.0).astype(bf16)
    return 128.0 * dot_nn(high, step) + dot_nn(low, step)


def running_columns(bins):
    size = bins.shape[1]
    high, low = split_bins(bins)
    step = jnp.where(iota((size, size), 1) <= iota((size, size), 0), 1.0, 0.0).astype(bf16)
    return 128.0 * dot_nt(step, high) + dot_nt(step, low)


def scale_column(rate_ref, total):
    count = rate_ref.shape[0]
    column = jnp.zeros((count, 1), f32)
    for head in range(count):
        column = jnp.where(iota((count, 1), 0) == head, rate_ref[head], column)
    return column * (-1.0 / total)


def weighted_sums(key_t, weight, both):
    width = key_t.shape[0]
    product = dot_nn(jnp.concatenate(split(key_t.astype(f32) * weight), 0), both)
    return product[:width] + product[width:]


def pack_gram(gram, decay):
    width = gram.shape[0]
    half = width // 2
    turned = pltpu.roll(gram[half:], half, 1)
    row, col = iota((half, width), 0), iota((half, width), 1)
    packed = jnp.where((col < half) & (row > col), turned, gram[:half])
    diagonal = jnp.sum(jnp.where(row == col, turned, 0.0), axis=0, keepdims=True)
    tail = jnp.where(iota((PAD, width), 0) == 0, diagonal, decay)
    return packed, tail


def unpack_gram(packed, diagonal):
    half, width = packed.shape
    turned = pltpu.roll(packed, half, 1)
    crossed = jnp.concatenate([packed, turned], 0).T
    row, col = iota((half, width), 0), iota((half, width), 1)
    top = jnp.where(row <= col, packed, crossed[:half])
    low_col = col - half
    bottom = jnp.where((low_col >= 0) & (row > low_col), turned, crossed[half:])
    bottom = jnp.where(row == low_col, pltpu.roll(jnp.broadcast_to(diagonal, (half, width)), half, 1), bottom)
    return jnp.concatenate([top, bottom], 0)


def sums_kernel(
    doc_ref, rate_ref, key_hbm, value_hbm, bins_hbm, gram_ref, memory_ref,
    weight_ref, decay_ref, both_ref, bins_ref, sems, bins_sem, *, total, heads, width,
):
    shard = key_hbm.shape[0]
    first = lax.axis_index("seq") * shard
    core = lax.axis_index("sub")
    bins_copy = pltpu.make_async_copy(bins_hbm, bins_ref, bins_sem)
    bins_copy.start()
    copies = []
    for i in range(heads):
        cols = pl.ds(pl.multiple_of((core * heads + i) * width, width), width)
        for part, source in enumerate((key_hbm, value_hbm)):
            target = both_ref.at[part, i]
            copies.append(pltpu.make_async_copy(source.at[:, cols], target, sems.at[i, part]))
            copies[-1].start()
    scale = scale_column(rate_ref, total)
    bins_copy.wait()
    cumulative = running_rows(bins_ref[...])
    last = cumulative[:, shard - 1 :]
    position = first + iota((1, shard), 1)
    end_doc = doc_of(doc_ref, first + shard - 1)
    weight_ref[...] = jnp.where(
        doc_of(doc_ref, position) == end_doc, jnp.exp(scale * (last - cumulative)), 0.0
    )
    through = end_doc == doc_of(doc_ref, first - 1)
    decay_ref[...] = jnp.broadcast_to(jnp.where(through, jnp.exp(scale * last), 0.0), decay_ref.shape)
    for i in range(heads):
        head = core * heads + i
        copies[2 * i].wait()
        copies[2 * i + 1].wait()
        key = both_ref[0, i]
        both = jnp.concatenate([key, both_ref[1, i]], 1)
        sums = weighted_sums(key.T, weight_ref[pl.ds(head, 1), :], both)
        state = jnp.concatenate(pack_gram(sums[:, :width], decay_ref[pl.ds(head, 1), :]), 0)
        gram_ref[i] = state
        memory_ref[i] = sums[:, width:]


def decay_line(gram_ref, i, half):
    return gram_ref[i, half + 1 : half + 2, :]


def include_kernel(own_ref, before_ref, own_gram, before_gram, out_ref, *, half, fresh):
    received = (lax.axis_index("seq") & 1) == 1
    for i in range(own_ref.shape[0]):
        decay = decay_line(own_gram, i, half)
        state = own_ref[i] + decay * before_ref[i]
        if own_ref.shape[1] != own_ref.shape[2]:
            over = decay_line(before_gram, i, half)
            over = jnp.where(received, over, 1.0) if fresh else over
            state = jnp.where(iota(state.shape, 0) > half, decay * over, state)
        out_ref[i] = state


def extend_kernel(before_ref, before_gram, *rest, half, bit, fresh):
    out_ref = rest[-1]
    first_received = (lax.axis_index("seq") & 1) == 1
    received = ((lax.axis_index("seq") >> bit) & 1) == 1
    for i in range(before_ref.shape[0]):
        arrived = rest[0][i]
        for other in rest[1:-1]:
            arrived = arrived + other[i]
        over = decay_line(before_gram, i, half)
        over = jnp.where(first_received, over, 1.0) if fresh else over
        state = before_ref[i] + over * arrived
        if before_ref.shape[1] != before_ref.shape[2]:
            passed = jnp.where(received, over * arrived[half + 1 : half + 2], over)
            state = jnp.where(iota(state.shape, 0) > half, passed, state)
        out_ref[i] = state


def prepare_kernel(
    doc_ref, rate_ref, query_ref, key_ref, value_ref, bins_ref,
    gate_ref, query_t_ref, key_t_ref, value_t_ref, within_ref, mid_gram_ref, mid_memory_ref, carried_ref,
    row_ref, column_ref, mid_ref, decay_ref, *, total, width,
):
    shard, rows = key_ref.shape[0], query_ref.shape[0]
    first = lax.axis_index("seq") * shard
    start = lax.axis_index("sub") * rows
    own = pl.ds(pl.multiple_of(start, rows), rows)
    before_doc = doc_of(doc_ref, first + start - 1)
    key_pos = first + start + iota((rows, 1), 0)
    own_pos = first + start + iota((1, rows), 1)
    own_doc = doc_of(doc_ref, own_pos)

    @pl.when(pl.program_id(0) == 0)
    def _():
        scale = scale_column(rate_ref, total)
        bins = bins_ref[...]
        cumulative = running_rows(bins)
        row_ref[...] = cumulative
        column_ref[...] = running_columns(bins)
        token = iota((1, shard), 1)
        before = jnp.sum(jnp.where(token == start - 1, cumulative, 0.0), axis=1, keepdims=True)
        mid_live = (token < start) & (doc_of(doc_ref, first + token) == before_doc)
        mid_ref[...] = jnp.where(
            mid_live, jnp.exp(scale * jnp.maximum(before - cumulative, 0.0)), 0.0
        )
        through = before_doc == doc_of(doc_ref, first - 1)
        decay_ref[...] = jnp.broadcast_to(
            jnp.where(through, jnp.exp(scale * before), 0.0), decay_ref.shape
        )
        carried_ref[...] = jnp.where(
            own_doc == before_doc, jnp.exp(scale * jnp.maximum(row_ref[:, own] - before, 0.0)), 0.0
        )

    allowed = (key_pos <= own_pos) & (doc_of(doc_ref, key_pos) == own_doc)
    columns = column_ref[own, :]
    for i in range(query_ref.shape[1] // width):
        head = pl.program_id(0) * PER_STEP + i
        scale = rate_ref[head] * (-1.0 / total)
        cols = slice(i * width, (i + 1) * width)
        key_t = key_ref[:, cols].T
        both = jnp.concatenate([key_ref[:, cols], value_ref[:, cols]], 1)
        sums = weighted_sums(key_t, mid_ref[pl.ds(head, 1), :], both)
        packed, tail = pack_gram(sums[:, :width], decay_ref[pl.ds(head, 1), :])
        mid_gram_ref[i, : width // 2, :] = packed
        mid_gram_ref[i, width // 2 :, :] = tail
        mid_memory_ref[i] = sums[:, width:]
        key_own = key_ref[own, cols]
        own_t = key_own.T
        query_t = query_ref[:, cols].T
        query_t_ref[i] = query_t
        key_t_ref[i] = own_t
        value_t_ref[i] = value_ref[own, cols].T
        column = jnp.sum(jnp.where(iota(columns.shape, 1) == head, columns, 0.0), axis=1, keepdims=True)
        gap = jnp.maximum(row_ref[pl.ds(head, 1), own] - column, 0.0)
        gate = jnp.where(allowed, jnp.exp(scale * gap), 0.0)
        gate_ref[i] = gate
        weighted = dot_nn(key_own, query_t) * gate
        within_ref[i] = dot_nn(jnp.concatenate([own_t, own_t], 1), jnp.concatenate(split(weighted), 0))


def solve_kernel(
    ridge_ref, key_ref, gate_ref, query_t_ref, key_t_ref, value_t_ref, within_ref, mid_ref, carried_ref,
    gram_ref, solution_ref, chunk_ref, *, cores, turn, width,
):
    rows = query_t_ref.shape[2]
    core = lax.axis_index("sub")
    steps = pl.num_programs(0)
    group = lax.rem(core + turn, cores)
    own = pl.ds(pl.multiple_of(core * rows, rows), rows)
    half = width // 2
    step = gram_ref.shape[0] // steps
    skip = pl.program_id(0) * step
    per_step = range(step)
    base = group * gram_ref.shape[0] + skip

    def row_sum(x):
        return jnp.sum(x, axis=0, keepdims=True)

    def head_program(i):
        head = base + i
        cols = pl.ds(pl.multiple_of(head * width, width), width)
        ridge = ridge_ref[head]
        carried = carried_ref[pl.ds(head, 1), :]
        decay = mid_ref[head, half + 1 : half + 2, :]
        packed = mid_ref[head, :half, :] + decay * gram_ref[skip + i, :half, :]
        diagonal = mid_ref[head, half : half + 1, :] + decay * gram_ref[skip + i, half : half + 1, :]
        high, low = split(unpack_gram(packed, diagonal))
        system = jnp.concatenate(
            [jnp.concatenate([high, low], 0), jnp.concatenate([high, jnp.zeros_like(low)], 0)], 1
        )
        key = key_ref[own, cols]
        keys = jnp.concatenate([key, key], 1)
        key_pair = jnp.concatenate([key_t_ref[head], key_t_ref[head]], 1)
        query_t = query_t_ref[head]
        direction = query_t.astype(f32)
        residual = direction
        energy = row_sum(direction * direction)
        result = None
        yield
        for iteration in range(ITERS):
            last = iteration == ITERS - 1
            if iteration == 0:
                product = dot_nn(system[:, :width], query_t)
            else:
                pair = jnp.concatenate(split(direction), 0)
                plain = dot_nn(keys, pair)
                product = dot_nn(system, pair)
            yield
            if iteration > 0:
                weighted = plain * gate_ref[head]
                if not last:
                    weighted_pair = jnp.concatenate(split(weighted), 0)
            earlier = carried * (product[:width] + product[width:]) + ridge * direction
            yield
            if iteration == 0:
                applied = earlier + within_ref[head]
            elif not last:
                within = dot_nn(key_pair, weighted_pair)
                yield
                applied = earlier + within
            if last:
                curvature = row_sum(plain * weighted) + row_sum(direction * earlier)
            else:
                curvature = row_sum(direction * applied)
            stepsize = energy / (curvature + guard)
            moved = stepsize * direction
            result = moved if iteration == 0 else result + moved
            if not last:
                residual = residual - stepsize * applied
                energy_next = row_sum(residual * residual)
                direction = residual + (energy_next / (energy + guard)) * direction
                energy = energy_next
            yield
        plain = dot_nn(keys, jnp.concatenate(split(result), 0))
        high, low = split(carried * result)
        solution_ref[skip + i] = jnp.concatenate([high.T, low.T], 1)
        yield
        weighted_pair = jnp.concatenate(split(plain * gate_ref[head]), 0)
        yield
        value_t = value_t_ref[head]
        chunk = dot_nn(jnp.concatenate([value_t, value_t], 1), weighted_pair)
        yield
        chunk_ref[skip + i] = chunk.T

    programs = [head_program(i) for i in per_step]
    running = []
    while programs or running:
        if programs:
            running.append(programs.pop(0))
        for program in list(running):
            if next(program, running) is running:
                running.remove(program)


def read_kernel(solution_ref, chunk_ref, mid_ref, mid_memory_ref, memory_ref, *rest, cores, turn, width):
    out_ref = rest[-1]
    half = width // 2
    heads = solution_ref.shape[0]
    base = lax.rem(lax.axis_index("sub") + turn, cores) * heads
    for i in range(heads):
        decay = mid_ref[base + i, half + 1 : half + 2, :]
        memory = mid_memory_ref[base + i] + decay * memory_ref[i]
        high, low = split(memory)
        pair = jnp.concatenate(
            [jnp.concatenate([high, high], 0), jnp.concatenate([low, jnp.zeros_like(low)], 0)], 1
        )
        product = dot_nn(solution_ref[i], pair)
        out = product[:, :width] + product[:, width:] + chunk_ref[i]
        out_ref[:, i * width : (i + 1) * width] = out.astype(out_ref.dtype)


def per_device(queries, key_vectors, value_vectors, gate_bins, doc_lengths, decay_rates, ridge_terms):
    head_count = decay_rates.shape[0]
    shard = key_vectors.shape[0]
    rows = queries.shape[0]
    width = key_vectors.shape[1] // head_count
    half = width // 2
    seq = lax.axis_size("seq")
    cores = lax.axis_size("sub")
    heads = head_count // cores
    total = shard * seq
    bins = gate_bins.T
    smem = pl.BlockSpec(memory_space=pltpu.SMEM)
    any_space = pl.BlockSpec(memory_space=pl.ANY)
    hbm = pl.BlockSpec(memory_space=pltpu.HBM)
    vmem = pl.BlockSpec(memory_space=pltpu.VMEM)

    def pinned(x):
        return pltpu.with_memory_space_constraint(x, pltpu.HBM)

    def full(*shape):
        return pl.BlockSpec(shape, lambda i: (0,) * len(shape))

    def call(kernel, grid, in_specs, out_specs, out_shape, scratch, name, cost, **options):
        return pl.pallas_call(
            kernel,
            grid=(grid,),
            in_specs=in_specs,
            out_specs=out_specs,
            scratch_shapes=scratch,
            out_shape=out_shape,
            name=name,
            cost_estimate=pl.CostEstimate(flops=cost, bytes_accessed=4 << 20, transcendentals=0),
            compiler_params=pltpu.CompilerParams(vmem_limit_bytes=VMEM),
            **options,
        )

    gram_sum, memory_sum = call(
        functools.partial(sums_kernel, total=total, heads=heads, width=width),
        1,
        [smem, smem, hbm, hbm, hbm],
        [vmem] * 2,
        [
            jax.ShapeDtypeStruct((heads, half + PAD, width), f32),
            jax.ShapeDtypeStruct((heads, width, width), f32),
        ],
        [
            pltpu.VMEM((head_count, shard), f32),
            pltpu.VMEM((head_count, width), f32),
            pltpu.VMEM((2, heads, shard, width), bf16),
            pltpu.VMEM((head_count, shard), jnp.int32),
            pltpu.SemaphoreType.DMA((heads, 2)),
            pltpu.SemaphoreType.DMA,
        ],
        "shard_sums",
        1 << 30,
    )(pinned(doc_lengths), pinned(decay_rates), pinned(key_vectors), pinned(value_vectors), pinned(bins))

    step = min(PER_STEP, heads)

    def head_block(*shape):
        return pl.BlockSpec((step, *shape), lambda i: (i,) + (0,) * len(shape))

    def step_block(count):
        return pl.BlockSpec((count, step * width), lambda i: (0, i))

    def per_head(*shape, dtype=f32):
        return jax.ShapeDtypeStruct((head_count, *shape), dtype)

    gate, query_t, key_t, value_t, within, mid_gram, mid_memory, carried = call(
        functools.partial(prepare_kernel, total=total, width=width),
        head_count // step,
        [smem, smem, step_block(rows), step_block(shard), step_block(shard), full(head_count, shard)],
        [
            head_block(rows, rows),
            head_block(width, rows),
            head_block(width, rows),
            head_block(width, rows),
            head_block(width, rows),
            head_block(half + PAD, width),
            head_block(width, width),
            full(head_count, rows),
        ],
        [
            per_head(rows, rows),
            per_head(width, rows, dtype=bf16),
            per_head(width, rows, dtype=bf16),
            per_head(width, rows, dtype=bf16),
            per_head(width, rows),
            per_head(half + PAD, width),
            per_head(width, width),
            per_head(rows),
        ],
        [
            pltpu.VMEM((head_count, shard), f32),
            pltpu.VMEM((shard, head_count), f32),
            pltpu.VMEM((head_count, shard), f32),
            pltpu.VMEM((head_count, width), f32),
        ],
        "prepare",
        4 << 30,
    )(doc_lengths, decay_rates, queries, key_vectors, value_vectors, bins)

    def after(x, *others):
        return lax.optimization_barrier((x, others))[0]

    def hops(x, size):
        got = []
        for offset in range(size):
            pairs = [
                (left + size - 1, left + size + offset)
                for left in range(0, seq, 2 * size)
                if left + size + offset < seq
            ]
            if pairs:
                got.append(lax.ppermute(x, "seq", pairs))
        return got

    def small(kernel, name, operands):
        return call(
            kernel,
            1,
            [vmem] * len(operands),
            vmem,
            jax.ShapeDtypeStruct(operands[0].shape, f32),
            [],
            name,
            1 << 20,
        )(*operands)

    def include(own, before, before_gram, fresh):
        kernel = functools.partial(include_kernel, half=half, fresh=fresh)
        return small(kernel, "include", [own, before, gram_sum, before_gram])

    def extend(before, before_gram, got, bit, fresh):
        kernel = functools.partial(extend_kernel, half=half, bit=bit, fresh=fresh)
        return small(kernel, "extend", [before, before_gram, *got])

    (gram_prior,), (memory_prior,) = hops(gram_sum, 1), hops(memory_sum, 1)
    gram_prior = after(gram_prior, carried)
    size, bit = 2, 1
    pending = None
    while size < seq:
        fresh = bit == 1
        if pending is not None:
            memory_prior = extend(*pending)
        gram_got = hops(include(gram_sum, gram_prior, gram_prior, fresh), size)
        memory_got = hops(include(memory_sum, memory_prior, gram_prior, fresh), size)
        pending = (memory_prior, gram_prior, memory_got, bit, fresh)
        gram_prior = extend(gram_prior, gram_prior, gram_got, bit, fresh)
        size, bit = 2 * size, bit + 1

    def memory_at(*ready):
        if pending is None:
            return memory_prior
        before, before_gram, got, *rest = pending
        return extend(before, before_gram, after(got, *ready), *rest)

    def swap(x):
        return lax.ppermute(x, "sub", [(i, (i + 1) % cores) for i in range(cores)])

    steps = heads // step
    solved = []
    for turn in range(cores):
        solved.append(
            call(
                functools.partial(solve_kernel, cores=cores, turn=turn, width=width),
                steps,
                [smem] + [vmem] * 9,
                [vmem] * 2,
                [
                    jax.ShapeDtypeStruct((heads, rows, 2 * width), bf16),
                    jax.ShapeDtypeStruct((heads, rows, width), f32),
                ],
                [],
                f"solve_{turn}",
                2 << 30,
            )(
                ridge_terms, key_vectors, gate, query_t, key_t, value_t, within, mid_gram, carried,
                gram_prior if turn == 0 else swap(gram_prior),
            )
        )

    memory_prior = memory_at(*solved)
    output = None
    for turn in range(cores):
        in_specs = [vmem] * 5
        operands = [*solved[turn], mid_gram, mid_memory, memory_prior if turn == 0 else swap(memory_prior)]
        aliases = {}
        if output is not None:
            aliases = {len(operands): 0}
            in_specs.append(any_space)
            operands.append(output)
        output = call(
            functools.partial(read_kernel, cores=cores, turn=turn, width=width),
            1,
            in_specs,
            pl.BlockSpec(
                (rows, heads * width), lambda i, turn=turn: (0, lax.rem(lax.axis_index("sub") + turn, cores))
            ),
            jax.ShapeDtypeStruct((rows, head_count * width), bf16),
            [],
            f"read_{turn}",
            1 << 28,
            input_output_aliases=aliases,
        )(*operands)
    return output


def solution(mesh):
    in_specs = (
        P(("rep", "seq", "sub"), "head"),
        P(("rep", "seq"), "head"),
        P(("rep", "seq"), "head"),
        P(("rep", "seq"), "head"),
        P("rep"),
        P("head"),
        P("head"),
    )
    out_specs = P(("rep", "seq", "sub"), "head")
    return jax.shard_map(per_device, mesh=mesh, in_specs=in_specs, out_specs=out_specs, check_vma=False)
```
